256 devices in a mesh: seq: 16 (over y, x), head: 16 (over z, core).
Axes of the slice: x: 4, y: 4, z: 8, core: 2. Of those that a mesh axis runs over, the one named last changes fastest.
Arguments:
- query_key: bfloat16 [2, 16384, 2048], P(None, 'seq', 'head'), may hold values from -6 to 6
- values: bfloat16 [2, 16384, 2048], P(None, 'seq', 'head'), may hold values from -6 to 6
- out_gate: bfloat16 [2, 16384, 2048], P(None, 'seq', 'head'), may hold values from -6 to 6
- log_gate: float32 [2, 16, 16384], P(None, 'head', 'seq'), may hold values from -1.3 to 0, as said below
- strength: float32 [2, 16, 16384], P(None, 'head', 'seq'), may hold values from 0 to 1, as said below
- norm_gain: float32 [128], replicated, may hold values from 0.1 to 1.9
Outputs:
- head_outputs: bfloat16 [2, 16384, 2048], P(None, 'seq', 'head')
The draws below stay inside these ranges and needn't reach their ends.
Inputs may be any that keep to these rules, and one draw needn't show every extreme that they name: log_gate is the natural logarithm of a per-token decay factor of each head's state. strength is the per-token write strength of each head.
All inputs are finite; a program needn't handle non-finite values.
Results may differ from the reference program's by a relative error of at most 0.001.
Values may be sent and summed in bfloat16 or wider, within the bound.
A program may use at most 64 MiB of HBM per device.

```python
from functools import partial
import jax
import jax.numpy as jnp
from jax import lax

DK = 128
DV = 128
REQUEST_COUNT = 2
GROUP = 64
VALUE_HEADS = 16
HK = 8
TOKEN_LENGTH = 16384


def head_plan(seed_key):
    plan_key = jax.random.fold_in(seed_key, 101)
    key_rank, key_slow, key_fast, key_wslow, key_wfast = jax.random.split(plan_key, 5)
    ranking = jax.random.permutation(key_rank, VALUE_HEADS)
    is_fast = ranking < VALUE_HEADS // 2
    slow_rate = jnp.exp(jax.random.uniform(key_slow, (VALUE_HEADS,), jnp.float32, jnp.log(0.05), jnp.log(0.4))) / TOKEN_LENGTH
    fast_rate = jax.random.uniform(key_fast, (VALUE_HEADS,), jnp.float32, 1.0 / 50.0, 1.0 / 30.0)
    decay_rate = jnp.where(is_fast, fast_rate, slow_rate)
    slow_write = jax.random.uniform(key_wslow, (VALUE_HEADS,), jnp.float32, 0.05, 0.3) * DK / TOKEN_LENGTH
    fast_write = jax.random.uniform(key_wfast, (VALUE_HEADS,), jnp.float32, 0.2, 0.45)
    write_base = jnp.where(is_fast, fast_write, slow_write)
    return (decay_rate, write_base)


def draw_log_gate(key, part):
    decay_rate, write_base = head_plan(key)
    own_key = jax.random.fold_in(key, 202)
    key_jit, position_key, logarithm_key = jax.random.split(own_key, 3)
    jitter = jax.random.uniform(key_jit, (REQUEST_COUNT, VALUE_HEADS, TOKEN_LENGTH), jnp.float32, 0.5, 2.0)
    spike_position = jax.random.randint(position_key, (REQUEST_COUNT, VALUE_HEADS, 2), 0, TOKEN_LENGTH)
    spike_logarithm_gate = jnp.log(jax.random.uniform(logarithm_key, (REQUEST_COUNT, VALUE_HEADS, 2), jnp.float32, 0.55, 0.8))
    token_places = jnp.arange(TOKEN_LENGTH)
    opening_section = jnp.where(token_places[None, None, :] == spike_position[:, :, 0:1], spike_logarithm_gate[:, :, 0:1], 0.0)
    closing_section = jnp.where(token_places[None, None, :] == spike_position[:, :, 1:2], spike_logarithm_gate[:, :, 1:2], 0.0)
    result = -decay_rate[None, :, None] * jitter + opening_section + closing_section
    return result.astype(jnp.float32)


def draw_strength(key, part):
    decay_rate, write_base = head_plan(key)
    own_key = jax.random.fold_in(key, 303)
    jitter = jax.random.uniform(own_key, (REQUEST_COUNT, VALUE_HEADS, TOKEN_LENGTH), jnp.float32, 0.5, 2.0)
    return (write_base[None, :, None] * jitter).astype(jnp.float32)


def block_levels(key, shape, pieces, smallest, top_value):
    loudness = 1.0
    for dim, blocks in pieces:
        heights = jax.random.uniform(jax.random.fold_in(jax.random.fold_in(key, 6), dim), (blocks,), jnp.float32, smallest / len(pieces), top_value / len(pieces))
        loudness = loudness * jnp.repeat(jnp.exp(heights), shape[dim] // blocks).reshape((-1,) + (1,) * (len(shape) - 1 - dim))
    return loudness


def noise(key, dims, deviation, most, cuts=(), held_as=jnp.bfloat16):
    drawn = deviation * jax.random.normal(key, dims, jnp.float32)
    if cuts:
        drawn = drawn * block_levels(key, dims, cuts, -0.22, 0.18)
    return jnp.clip(drawn, -most, most).astype(held_as)


def setup_inputs(seed: int = 0) -> dict:
    key_list = jax.random.split(jax.random.key(seed), 7)
    query_key = noise(key_list[0], (REQUEST_COUNT, TOKEN_LENGTH, HK * 2 * DK), 1.0, 6.0, ((1, 16), (2, 16)))
    values = noise(key_list[1], (REQUEST_COUNT, TOKEN_LENGTH, VALUE_HEADS * DV), 1.0, 6.0, ((1, 16), (2, 16)))
    out_gate = noise(key_list[2], (REQUEST_COUNT, TOKEN_LENGTH, VALUE_HEADS * DV), 1.0, 6.0, ((1, 16), (2, 16)))
    log_gate = draw_log_gate(jax.random.fold_in(key_list[6], 71), 0)
    strength = draw_strength(jax.random.fold_in(key_list[6], 71), 0)
    norm_gain = jnp.clip(1.0 + 0.18 * jax.random.normal(key_list[5], (DV,), jnp.float32), 0.1, 1.9)
    return dict(query_key=query_key, values=values, out_gate=out_gate, log_gate=log_gate, strength=strength, norm_gain=norm_gain)


def mult(form, left, right):
    return jnp.einsum(form, left, right, precision=lax.Precision.HIGHEST)

def normalize(vectors):
    return vectors / jnp.sqrt(lax.optimization_barrier(jnp.sum(vectors * vectors, axis=-1, keepdims=True)) + 1e-06)

def solve_lower(system, right_side):
    leading = system.shape[:-2]
    flat_sys = system.reshape((-1,) + system.shape[-2:])
    flat_rhs = right_side.reshape((-1,) + right_side.shape[-2:])
    solver = partial(jax.scipy.linalg.solve_triangular, lower=True, unit_diagonal=True)
    solved = jax.vmap(solver)(flat_sys, flat_rhs)
    return solved.reshape(leading + solved.shape[-2:])

def group_terms(queries, keys, vals, log_steps, writes):
    span = log_steps.shape[-1]
    cumulative = jnp.cumsum(log_steps, axis=-1)
    token_places = jnp.arange(span)
    causal = token_places[:, None] >= token_places[None, :]
    strict = token_places[:, None] > token_places[None, :]
    spread = cumulative[..., :, None] - cumulative[..., None, :]
    decays = jnp.where(causal, jnp.exp(jnp.where(causal, spread, 0.0)), 0.0)
    key_gram = mult('...td,...sd->...ts', keys, keys)
    lower_part = jnp.where(strict, decays * key_gram * writes[..., None, :], 0.0)
    system = lower_part + jnp.eye(span, dtype=jnp.float32)
    growth = jnp.exp(cumulative)
    right_side = jnp.concatenate([vals, growth[..., None] * keys], axis=-1)
    solved = solve_lower(system, right_side)
    val_width = vals.shape[-1]
    fresh_vals = solved[..., :val_width]
    key_mix = solved[..., val_width:]
    mixing = jnp.where(causal, decays * mult('...td,...sd->...ts', queries, keys) * writes[..., None, :], 0.0)
    query_lead = growth[..., None] * queries
    key_tail = keys * (jnp.exp(cumulative[..., -1:] - cumulative) * writes)[..., None]
    group_decay = growth[..., -1]
    return (fresh_vals, key_mix, mixing, query_lead, key_tail, group_decay)

def gated_norm(raw, out_gate, norm_gain):
    mean_square = lax.optimization_barrier(jnp.mean(raw * raw, axis=-1, keepdims=True))
    gate_val = out_gate.astype(jnp.float32)
    scaled = raw / jnp.sqrt(mean_square + 1e-06) * norm_gain.astype(jnp.float32)
    return (scaled * gate_val * jax.nn.sigmoid(gate_val)).astype(jnp.bfloat16)

def advance(state, inputs):
    fresh_vals, key_mix, mixing, query_lead, key_tail, group_decay = inputs
    update = fresh_vals - mult('cd,de->ce', key_mix, state)
    output = mult('cd,de->ce', query_lead, state) + mult('cs,se->ce', mixing, update)
    state = group_decay * state + mult('cd,ce->de', key_tail, update)
    return (state, output)

def reference(query_key, values, out_gate, log_gate, strength, norm_gain):
    num_blocks = TOKEN_LENGTH // GROUP

    def one_head(flat_index):
        batch_idx = flat_index // VALUE_HEADS
        head_idx = flat_index % VALUE_HEADS
        anchor = flat_index * 0
        column = head_idx // 2 * (2 * DK)
        queries = lax.dynamic_slice(query_key, (batch_idx, anchor, column), (1, TOKEN_LENGTH, DK))[0]
        keys = lax.dynamic_slice(query_key, (batch_idx, anchor, column + DK), (1, TOKEN_LENGTH, DK))[0]
        queries = normalize(queries.astype(jnp.float32))
        keys = normalize(keys.astype(jnp.float32))
        vals = lax.dynamic_slice(values, (batch_idx, anchor, head_idx * DV), (1, TOKEN_LENGTH, DV))[0].astype(jnp.float32)
        gates = lax.dynamic_slice(out_gate, (batch_idx, anchor, head_idx * DV), (1, TOKEN_LENGTH, DV))[0]
        log_steps = lax.dynamic_slice(log_gate, (batch_idx, head_idx, anchor), (1, 1, TOKEN_LENGTH))[0, 0]
        writes = lax.dynamic_slice(strength, (batch_idx, head_idx, anchor), (1, 1, TOKEN_LENGTH))[0, 0]
        terms = group_terms(queries.reshape(num_blocks, GROUP, DK), keys.reshape(num_blocks, GROUP, DK), vals.reshape(num_blocks, GROUP, DV), log_steps.reshape(num_blocks, GROUP), writes.reshape(num_blocks, GROUP))
        start_state = jnp.zeros((DK, DV), jnp.float32)
        final_state, outputs = lax.scan(advance, start_state, terms)
        raw = outputs.reshape(TOKEN_LENGTH, DV)
        return gated_norm(raw, gates, norm_gain)
    heads = lax.map(one_head, jnp.arange(REQUEST_COUNT * VALUE_HEADS, dtype=jnp.int32))
    heads = heads.reshape(REQUEST_COUNT, VALUE_HEADS, TOKEN_LENGTH, DV).transpose(0, 2, 1, 3)
    return heads.reshape(REQUEST_COUNT, TOKEN_LENGTH, VALUE_HEADS * DV)
```

```python
import jax
import jax.numpy as jnp
from jax import lax
from jax.experimental import pallas as pl
from jax.experimental.pallas import tpu as pltpu
from jax.sharding import PartitionSpec as P

MESH = pl.DeviceIdType.MESH
C = 128
D = 128
X = 4
F32 = jnp.float32
BF16 = jnp.bfloat16


def split(a):
    hi = a.astype(BF16)
    return hi, (a - hi.astype(F32)).astype(BF16)


def mm(a, b):
    return lax.dot_general(a, b, (((1,), (0,)), ((), ())), preferred_element_type=F32)


def mm_t(a, b):
    return lax.dot_general(a, b, (((1,), (1,)), ((), ())), preferred_element_type=F32)


def dot3(a, b, mul=mm):
    (ah, al), (bh, bl) = a, b
    n = ah.shape[0]
    both = mul(jnp.concatenate([ah, al], axis=0), bh)
    return both[:n] + (both[n:] + mul(ah, bl))


def dot2(a, b):
    ah, al = a
    n = ah.shape[0]
    both = mm(jnp.concatenate([ah, al], axis=0), b)
    return both[:n] + both[n:]


def iota(shape, dim):
    return lax.broadcasted_iota(jnp.int32, shape, dim)


def inverse(low):
    lanes8 = iota((8, C), 1)
    rows8 = iota((8, C), 0)
    rows = []
    for n in range(C // 8):
        part = low[8 * n : 8 * n + 8]
        inv = jnp.where(lanes8 == rows8 + 8 * n, 1.0, 0.0).astype(F32)
        for j in range(7):
            inv = inv - part[:, 8 * n + j : 8 * n + j + 1] * inv[j : j + 1]
        rows.append(inv)
    b = 8
    while b < C:
        g = b // 8
        pairs = C // (2 * b)
        lane_b = iota((b, C), 1)
        off, odd = [], []
        for p in range(pairs):
            r0 = (2 * p + 1) * b
            inside = (lane_b >= 2 * p * b) & (lane_b < r0)
            off.append(jnp.where(inside, low[r0 : r0 + b], 0.0))
            odd += rows[(2 * p + 1) * g : (2 * p + 2) * g]
        off = jnp.concatenate(off, axis=0)
        odd = jnp.concatenate(odd, axis=0)
        full = jnp.concatenate(rows, axis=0)
        y = dot3(split(off), split(full))
        zero = jnp.zeros((b, C), F32)
        spread = []
        for p in range(pairs):
            spread += [zero, y[p * b : (p + 1) * b]]
        spread = jnp.concatenate(spread, axis=0)
        odd = odd - dot3(split(odd), split(spread))
        for p in range(pairs):
            for i in range(g):
                at = (p * g + i) * 8
                rows[(2 * p + 1) * g + i] = odd[at : at + 8]
        b *= 2
    return jnp.concatenate(rows, axis=0)


def kernel(
    chunks,
    qk_hbm,
    values_ref,
    gate_ref,
    log_ref,
    write_ref,
    gain_ref,
    out_ref,
    qk,
    cum,
    decay,
    wh,
    wl,
    xh,
    xl,
    qah,
    qal,
    ob,
    agat,
    bown,
    bgat,
    srow,
    snext,
    sout,
    sin,
    local_sem,
    send_sem,
    recv_sem,
):
    seq = lax.axis_index("seq")
    head = lax.axis_index("head")
    col = lax.rem(seq, X)
    row = seq // X
    base = row * X
    rows = X
    right = base + lax.rem(col + 1, X)
    left = base + lax.rem(col + X - 1, X)
    across = base + lax.rem(col + 2, X)
    below = lax.rem(row + 1, rows) * X + col
    above = lax.rem(row + rows - 1, rows) * X + col
    parity = lax.rem(head, 2)
    partner = head + 1 - 2 * parity

    barrier = pltpu.get_barrier_semaphore()
    pl.semaphore_signal(barrier, inc=1, device_id={"head": partner}, device_id_type=MESH)
    for other in (right, left, across, below, above):
        pl.semaphore_signal(barrier, inc=1, device_id={"seq": other}, device_id_type=MESH)
    own = pltpu.make_async_copy(qk_hbm, qk.at[parity], local_sem)
    own.start()

    tri = jnp.where(iota((C, C), 0) <= iota((C, C), 1), 1.0, 0.0).astype(F32)
    for r in range(2):
        cum[r] = lax.dot_general(
            log_ref[r],
            tri,
            (((1,), (0,)), ((), ())),
            precision=lax.Precision.HIGHEST,
            preferred_element_type=F32,
        )

    pl.semaphore_wait(barrier, 6)

    def remote(src, dst, index, target, axis="seq"):
        return pltpu.make_async_remote_copy(
            src_ref=src,
            dst_ref=dst,
            send_sem=send_sem.at[index],
            recv_sem=recv_sem.at[index],
            device_id={axis: target},
            device_id_type=MESH,
        )

    swap = remote(qk_hbm, qk.at[parity], 0, partner, "head")
    swap.start()

    eye = iota((C, C), 0) == iota((C, C), 1)
    causal = iota((C, C), 0) >= iota((C, C), 1)
    strict = iota((C, C), 0) > iota((C, C), 1)
    ident = jnp.where(eye, 1.0, 0.0).astype(F32)
    for r in range(2):
        xh[r, 0] = jnp.concatenate([ident, jnp.zeros((C, D), F32)], axis=1).astype(BF16)
        xl[r, 0] = jnp.zeros((C, 2 * D), BF16)

    own.wait()
    swap.wait()

    def first(r, c):
        span = pl.ds(pl.multiple_of(c * C, C), C)
        k = qk[1, r, span, :]
        v = values_ref[r, span, :]
        cum_row = cum[r, pl.ds(c, 1), :]
        w_row = write_ref[r, pl.ds(c, 1), :]
        gram = mm_t(k, k)
        squares = jnp.sum(jnp.where(eye, gram, 0.0), axis=0, keepdims=True)
        rn_row = lax.rsqrt(squares + 1e-06)
        last = cum_row[:, C - 1 : C]
        tail_row = jnp.exp(last - cum_row) * w_row * rn_row
        packed = jnp.concatenate([cum_row, rn_row, tail_row, jnp.zeros((5, C), F32)], axis=0)
        cols = packed.T
        cum_col, rn_col, tail_col = cols[:, 0:1], cols[:, 1:2], cols[:, 2:3]
        spread = jnp.exp(jnp.where(causal, cum_col - cum_row, -1e30)) * (w_row * rn_row)
        decay[r, c] = spread
        low = jnp.where(strict, spread * gram * rn_col, 0.0)
        inv = inverse(low)
        scaled = inv * (jnp.exp(cum_row) * rn_row)
        mix = jnp.concatenate([dot2(split(scaled), k), dot2(split(inv), v)], axis=1)
        mh, ml = split(mix)
        wh[r, c] = mh
        wl[r, c] = ml
        uh, ul = split(mix * tail_col)
        kt = k.T
        ab = mm(kt, uh) + mm(kt, ul)
        step = ident * jnp.exp(last) - ab[:, :D]
        nxt = dot3(split(step), (xh[r, c], xl[r, c]))
        nxt = nxt + jnp.concatenate([jnp.zeros((D, D), F32), ab[:, D:]], axis=1)
        return nxt

    def first_loop(c, _):
        for r in range(2):
            nxt = first(r, c)
            nh, nl = split(nxt)
            xh[r, c + 1] = nh
            xl[r, c + 1] = nl
        return 0

    lax.fori_loop(0, chunks, first_loop, 0)

    sends = []

    def send(*args):
        copy = remote(*args)
        copy.start()
        sends.append(copy)
        return copy

    for r in range(2):
        full = xh[r, chunks].astype(F32) + xl[r, chunks].astype(F32)
        agat[col, r] = full[:, :D]
        bown[r] = full[:, D:].T
    for r in range(2):
        mine = agat.at[col, r]
        send(mine, mine, 1 + r, right)
        send(mine, mine, 3 + r, left)
    block = D // X
    for o, target in ((1, right), (2, across), (3, left)):
        there = pl.ds(pl.multiple_of(lax.rem(col + o, X) * block, block), block)
        send(bown.at[:, there, :], bgat.at[col], 6 + o, target)
    here = pl.ds(pl.multiple_of(col * block, block), block)
    bgat[col] = bown[:, here, :]

    def second(r, c):
        span = pl.ds(pl.multiple_of(c * C, C), C)
        q = qk[0, r, span, :]
        k = qk[1, r, span, :]
        cum_row = cum[r, pl.ds(c, 1), :]
        packed = jnp.broadcast_to(jnp.exp(cum_row), (8, C))
        grow = packed.T[:, 0:1]
        mixing = decay[r, c] * mm_t(q, k)
        both = dot3(split(mixing), (wh[r, c], wl[r, c]))
        lead = grow * q.astype(F32) - both[:, :D]
        res = dot3(split(lead), (xh[r, c], xl[r, c]))
        ah, al = split(res[:, :D])
        qah[r, span, :] = ah
        qal[r, span, :] = al
        ob[r, span, :] = both[:, D:] + res[:, D:]

    def second_loop(c, _):
        for r in range(2):
            second(r, c)
        return 0

    half = chunks // 2
    lax.fori_loop(0, half, second_loop, 0)

    before = lax.rem(col + X - 1, X)
    after = lax.rem(col + 1, X)
    far = lax.rem(col + 2, X)

    def arrival(ref, index):
        return pltpu.make_async_remote_copy(
            src_ref=ref,
            dst_ref=ref,
            send_sem=send_sem.at[index],
            recv_sem=recv_sem.at[index],
            device_id={"seq": right},
            device_id_type=MESH,
        )

    arrival(agat.at[before, 0], 1).wait_recv()
    send(agat.at[before, 0], agat.at[before, 0], 5, right)
    arrival(agat.at[after, 1], 4).wait_recv()
    send(agat.at[after, 1], agat.at[after, 1], 6, left)

    lax.fori_loop(half, chunks, second_loop, 0)

    arrival(agat.at[before, 1], 2).wait_recv()
    arrival(agat.at[after, 0], 3).wait_recv()
    for o in (1, 2, 3):
        arrival(bgat.at[lax.rem(col + X - o, X)], 6 + o).wait_recv()
    arrival(agat.at[far, 0], 5).wait_recv()
    arrival(agat.at[far, 1], 6).wait_recv()

    gains = []
    for r in range(2):
        steps = [split(agat[i, r]) for i in range(X)]
        lead = [None, steps[0]]
        offset = [jnp.zeros((block, D), F32), bgat[0, r]]
        for i in range(1, X):
            lead.append(split(dot3(steps[i], lead[i])))
            offset.append(dot3(split(offset[i]), steps[i], mm_t) + bgat[i, r])
        gains.append((lead, offset))

    @pl.when(row == 0)
    def _():
        srow[...] = jnp.zeros_like(srow)

    @pl.when(row > 0)
    def _():
        arrival(srow, 10).wait_recv()

    state = [split(srow[r]) for r in range(2)]
    for r in range(2):
        lead, offset = gains[r]
        snext[r] = dot3(state[r], lead[X], mm_t) + offset[X]
    down = remote(snext, srow, 10, below)

    @pl.when(row < rows - 1)
    def _():
        down.start()

    for r in range(2):
        lead, offset = gains[r]
        sout[0, r] = srow[r]
        for i in range(1, X):
            sout[i, r] = dot3(state[r], lead[i], mm_t) + offset[i]
    for o, target in ((1, right), (2, across), (3, left)):
        send(sout.at[lax.rem(col + o, X)], sin.at[:, here, :], 10 + o, target)
    sin[:, here, :] = sout[col]
    for o in (1, 2, 3):
        there = pl.ds(pl.multiple_of(lax.rem(col + X - o, X) * block, block), block)
        arrival(sin.at[:, there, :], 10 + o).wait_recv()

    gain = gain_ref[...]

    for r in range(2):
        state_in = split(sin[r])

        def last_loop(c, _):
            span = pl.ds(pl.multiple_of(c * C, C), C)
            raw = ob[r, span, :] + dot3((qah[r, span, :], qal[r, span, :]), state_in, mm_t)
            qf = qk[0, r, span, :].astype(F32)
            raw = raw * lax.rsqrt(jnp.sum(qf * qf, axis=1, keepdims=True) + 1e-06)
            mean = jnp.sum(raw * raw, axis=1, keepdims=True) * (1.0 / D)
            g = gate_ref[r, span, :].astype(F32)
            silu = g / (1.0 + jnp.exp(-g))
            out_ref[r, span, :] = (raw * lax.rsqrt(mean + 1e-06) * gain * silu).astype(BF16)
            return 0

        lax.fori_loop(0, chunks, last_loop, 0)

    for copy in sends:
        copy.wait_send()

    @pl.when(row < rows - 1)
    def _():
        down.wait_send()


def body(query_key, values, out_gate, log_gate, strength, norm_gain):
    requests, length, _ = values.shape
    chunks = length // C
    vmem = pl.BlockSpec(memory_space=pltpu.VMEM)
    wide = (requests, chunks, C, 2 * D)
    block = D // X

    def call(*args):
        return pl.pallas_call(
            lambda *refs: kernel(chunks, *refs),
            out_shape=jax.ShapeDtypeStruct(values.shape, BF16),
            in_specs=[pl.BlockSpec(memory_space=pl.ANY)] + [vmem] * 5,
            out_specs=vmem,
            scratch_shapes=[
                pltpu.VMEM((2,) + query_key.shape, BF16),
                pltpu.VMEM((requests, chunks, C), F32),
                pltpu.VMEM((requests, chunks, C, C), F32),
                pltpu.VMEM(wide, BF16),
                pltpu.VMEM(wide, BF16),
                pltpu.VMEM((requests, chunks + 1, D, 2 * D), BF16),
                pltpu.VMEM((requests, chunks + 1, D, 2 * D), BF16),
                pltpu.VMEM((requests, length, D), BF16),
                pltpu.VMEM((requests, length, D), BF16),
                pltpu.VMEM((requests, length, D), F32),
                pltpu.VMEM((X, requests, D, D), F32),
                pltpu.VMEM((requests, D, D), F32),
                pltpu.VMEM((X, requests, block, D), F32),
                pltpu.VMEM((requests, block, D), F32),
                pltpu.VMEM((requests, block, D), F32),
                pltpu.VMEM((X, requests, block, D), F32),
                pltpu.VMEM((requests, D, D), F32),
                pltpu.SemaphoreType.DMA,
                pltpu.SemaphoreType.DMA((14,)),
                pltpu.SemaphoreType.DMA((14,)),
            ],
            compiler_params=pltpu.CompilerParams(collective_id=0, has_side_effects=True),
        )(*args)

    return call(
        query_key,
        values,
        out_gate,
        log_gate.reshape(requests, chunks, C),
        strength.reshape(requests, chunks, C),
        norm_gain.reshape(1, D),
    )


def solution(mesh):
    return jax.shard_map(
        body,
        mesh=mesh,
        in_specs=(
            P(None, "seq", "head"),
            P(None, "seq", "head"),
            P(None, "seq", "head"),
            P(None, "head", "seq"),
            P(None, "head", "seq"),
            P(),
        ),
        out_specs=P(None, "seq", "head"),
        check_vma=False,
    )
```

```python
import jax
import jax.numpy as jnp
from jax import lax
from jax.experimental import pallas as pl
from jax.experimental.pallas import tpu as pltpu
from jax.sharding import PartitionSpec as P

MESH = pl.DeviceIdType.MESH
C = 128
D = 128
X = 4
GROUP = 2
F32 = jnp.float32
BF16 = jnp.bfloat16


def split(a):
    hi = a.astype(BF16)
    return hi, (a - hi.astype(F32)).astype(BF16)


def mm(a, b):
    return lax.dot_general(a, b, (((1,), (0,)), ((), ())), preferred_element_type=F32)


def mm_t(a, b):
    return lax.dot_general(a, b, (((1,), (1,)), ((), ())), preferred_element_type=F32)


def dot3(a, b, mul=mm):
    (ah, al), (bh, bl) = a, b
    n = ah.shape[0]
    both = mul(jnp.concatenate([ah, al], axis=0), bh)
    return both[:n] + (both[n:] + mul(ah, bl))


def dot2(a, b):
    ah, al = a
    n = ah.shape[0]
    both = mm(jnp.concatenate([ah, al], axis=0), b)
    return both[:n] + both[n:]


def iota(shape, dim):
    return lax.broadcasted_iota(jnp.int32, shape, dim)


def inverse(lows):
    lanes8 = iota((8, C), 1)
    rows8 = iota((8, C), 0)
    group8 = lanes8 // 8
    count = range(len(lows))
    packs = []
    for m in count:
        parts = [jnp.where(group8 == n, lows[m][8 * n : 8 * n + 8], 0.0) for n in range(C // 8)]
        while len(parts) > 1:
            parts = [parts[i] + parts[i + 1] for i in range(0, len(parts), 2)]
        packs.append(parts[0])
    small = [jnp.where(lanes8 - 8 * group8 == rows8, 1.0, 0.0).astype(F32)] * len(lows)
    for j in range(7):
        spot = 8 * group8 + j
        heads = [jnp.take_along_axis(packs[m], spot, axis=1, mode="promise_in_bounds") for m in count]
        small = [small[m] - heads[m] * small[m][j : j + 1] for m in count]
    rows = [[jnp.where(group8 == n, small[m], 0.0) for n in range(C // 8)] for m in count]
    b = 8
    while b < C:
        g = b // 8
        pairs = C // (2 * b)
        lane_b = iota((b, C), 1)
        zero = jnp.zeros((b, C), F32)
        offs, odds, fulls = [], [], []
        for m in count:
            off, odd = [], []
            for p in range(pairs):
                r0 = (2 * p + 1) * b
                inside = (lane_b >= 2 * p * b) & (lane_b < r0)
                off.append(jnp.where(inside, lows[m][r0 : r0 + b], 0.0))
                odd += rows[m][(2 * p + 1) * g : (2 * p + 2) * g]
            offs.append(split(jnp.concatenate(off, axis=0)))
            odds.append(jnp.concatenate(odd, axis=0))
            fulls.append(split(jnp.concatenate(rows[m], axis=0)))
        ys = [dot3(offs[m], fulls[m]) for m in count]
        spreads = []
        for m in count:
            spread = []
            for p in range(pairs):
                spread += [zero, ys[m][p * b : (p + 1) * b]]
            spreads.append(split(jnp.concatenate(spread, axis=0)))
        news = [odds[m] - dot3(split(odds[m]), spreads[m]) for m in count]
        for m in count:
            for p in range(pairs):
                for i in range(g):
                    at = (p * g + i) * 8
                    rows[m][(2 * p + 1) * g + i] = news[m][at : at + 8]
        b *= 2
    return [jnp.concatenate(rows[m], axis=0) for m in count]


def kernel(
    chunks,
    qk_hbm,
    values_ref,
    gate_ref,
    log_ref,
    write_ref,
    gain_ref,
    out_ref,
    qk,
    cum,
    decay,
    wh,
    wl,
    step_h,
    step_l,
    add,
    xh,
    xl,
    qah,
    qal,
    ob,
    agat,
    bown,
    bgat,
    srow,
    snext,
    sout,
    sin,
    local_sem,
    send_sem,
    recv_sem,
):
    seq = lax.axis_index("seq")
    head = lax.axis_index("head")
    col = lax.rem(seq, X)
    row = seq // X
    base = row * X
    rows = X
    right = base + lax.rem(col + 1, X)
    left = base + lax.rem(col + X - 1, X)
    across = base + lax.rem(col + 2, X)
    below = lax.rem(row + 1, rows) * X + col
    above = lax.rem(row + rows - 1, rows) * X + col
    parity = lax.rem(head, 2)
    partner = head + 1 - 2 * parity

    barrier = pltpu.get_barrier_semaphore()
    pl.semaphore_signal(barrier, inc=1, device_id={"head": partner}, device_id_type=MESH)
    for other in (right, left, across, below, above):
        pl.semaphore_signal(barrier, inc=1, device_id={"seq": other}, device_id_type=MESH)
    own = pltpu.make_async_copy(qk_hbm, qk.at[parity], local_sem)
    own.start()

    tri = jnp.where(iota((C, C), 0) <= iota((C, C), 1), 1.0, 0.0).astype(F32)
    for r in range(2):
        cum[r] = lax.dot_general(
            log_ref[r],
            tri,
            (((1,), (0,)), ((), ())),
            precision=lax.Precision.HIGHEST,
            preferred_element_type=F32,
        )

    pl.semaphore_wait(barrier, 6)

    def remote(src, dst, index, target, axis="seq"):
        return pltpu.make_async_remote_copy(
            src_ref=src,
            dst_ref=dst,
            send_sem=send_sem.at[index],
            recv_sem=recv_sem.at[index],
            device_id={axis: target},
            device_id_type=MESH,
        )

    swap = remote(qk_hbm, qk.at[parity], 0, partner, "head")
    swap.start()

    eye = iota((C, C), 0) == iota((C, C), 1)
    causal = iota((C, C), 0) >= iota((C, C), 1)
    strict = iota((C, C), 0) > iota((C, C), 1)
    ident = jnp.where(eye, 1.0, 0.0).astype(F32)
    for r in range(2):
        xh[r, 0] = jnp.concatenate([ident, jnp.zeros((C, D), F32)], axis=1).astype(BF16)
        xl[r, 0] = jnp.zeros((C, 2 * D), BF16)

    own.wait()
    swap.wait()

    def first(batch):
        count = range(len(batch))
        ks, lows, cum_rows, rn_rows, tails, lasts = [], [], [], [], [], []
        for r, c in batch:
            k = qk[1, r, pl.ds(pl.multiple_of(c * C, C), C), :]
            ks.append(k)
        grams = [mm_t(k, k) for k in ks]
        for m in count:
            r, c = batch[m]
            cum_row = cum[r, pl.ds(c, 1), :]
            w_row = write_ref[r, pl.ds(c, 1), :]
            gram = grams[m]
            squares = jnp.sum(jnp.where(eye, gram, 0.0), axis=0, keepdims=True)
            rn_row = lax.rsqrt(squares + 1e-06)
            last = cum_row[:, C - 1 : C]
            tail_row = jnp.exp(last - cum_row) * w_row * rn_row
            packed = jnp.concatenate([cum_row, rn_row, tail_row, jnp.zeros((5, C), F32)], axis=0)
            cols = packed.T
            spread = jnp.exp(jnp.where(causal, cols[:, 0:1] - cum_row, -1e30)) * (w_row * rn_row)
            decay[r, c] = spread
            lows.append(jnp.where(strict, spread * gram * cols[:, 1:2], 0.0))
            cum_rows.append(cum_row)
            rn_rows.append(rn_row)
            tails.append(cols[:, 2:3])
            lasts.append(last)
        invs = inverse(lows)
        scaleds = [split(invs[m] * (jnp.exp(cum_rows[m]) * rn_rows[m])) for m in count]
        invs = [split(invs[m]) for m in count]
        mixes = []
        for m in count:
            r, c = batch[m]
            v = values_ref[r, pl.ds(pl.multiple_of(c * C, C), C), :]
            mixes.append(jnp.concatenate([dot2(scaleds[m], ks[m]), dot2(invs[m], v)], axis=1))
        for m in count:
            r, c = batch[m]
            mh, ml = split(mixes[m])
            wh[r, c] = mh
            wl[r, c] = ml
            uh, ul = split(mixes[m] * tails[m])
            kt = ks[m].T
            ab = mm(kt, uh) + mm(kt, ul)
            sh, sl = split(ident * jnp.exp(lasts[m]) - ab[:, :D])
            step_h[r, c] = sh
            step_l[r, c] = sl
            add[r, c] = ab[:, D:]

    def scan(r, c):
        nxt = dot3((step_h[r, c], step_l[r, c]), (xh[r, c], xl[r, c]))
        nxt = nxt + jnp.concatenate([jnp.zeros((D, D), F32), add[r, c]], axis=1)
        nh, nl = split(nxt)
        xh[r, c + 1] = nh
        xl[r, c + 1] = nl

    first([(r, c) for c in range(GROUP) for r in range(2)])

    def first_loop(i, _):
        for j in range(GROUP):
            for r in range(2):
                scan(r, (i - 1) * GROUP + j)
        first([(r, i * GROUP + c) for c in range(GROUP) for r in range(2)])
        return 0

    lax.fori_loop(1, chunks // GROUP, first_loop, 0)
    for j in range(GROUP):
        for r in range(2):
            scan(r, chunks - GROUP + j)

    sends = []

    def send(*args):
        copy = remote(*args)
        copy.start()
        sends.append(copy)
        return copy

    for r in range(2):
        full = xh[r, chunks].astype(F32) + xl[r, chunks].astype(F32)
        agat[col, r] = full[:, :D]
        bown[r] = full[:, D:].T
    for r in range(2):
        mine = agat.at[col, r]
        send(mine, mine, 1 + r, right)
        send(mine, mine, 3 + r, left)
    block = D // X
    for o, target in ((1, right), (2, across), (3, left)):
        there = pl.ds(pl.multiple_of(lax.rem(col + o, X) * block, block), block)
        send(bown.at[:, there, :], bgat.at[col], 6 + o, target)
    here = pl.ds(pl.multiple_of(col * block, block), block)
    bgat[col] = bown[:, here, :]

    def second(batch):
        count = range(len(batch))
        spans = [pl.ds(pl.multiple_of(c * C, C), C) for _, c in batch]
        qs = [qk[0, batch[m][0], spans[m], :] for m in count]
        prods = [mm_t(qs[m], qk[1, batch[m][0], spans[m], :]) for m in count]
        grows, boths, leads = [], [], []
        for r, c in batch:
            packed = jnp.broadcast_to(jnp.exp(cum[r, pl.ds(c, 1), :]), (8, C))
            grows.append(packed.T[:, 0:1])
        mixings = [split(decay[batch[m]] * prods[m]) for m in count]
        boths = [dot3(mixings[m], (wh[batch[m]], wl[batch[m]])) for m in count]
        leads = [split(grows[m] * qs[m].astype(F32) - boths[m][:, :D]) for m in count]
        for m in count:
            r, c = batch[m]
            res = dot3(leads[m], (xh[r, c], xl[r, c]))
            ah, al = split(res[:, :D])
            qah[r, spans[m], :] = ah
            qal[r, spans[m], :] = al
            ob[r, spans[m], :] = boths[m][:, D:] + res[:, D:]

    def second_loop(i, _):
        second([(r, i * GROUP + j) for j in range(GROUP) for r in range(2)])
        return 0

    half = chunks // GROUP // 2
    lax.fori_loop(0, half, second_loop, 0)

    before = lax.rem(col + X - 1, X)
    after = lax.rem(col + 1, X)
    far = lax.rem(col + 2, X)

    def arrival(ref, index):
        return pltpu.make_async_remote_copy(
            src_ref=ref,
            dst_ref=ref,
            send_sem=send_sem.at[index],
            recv_sem=recv_sem.at[index],
            device_id={"seq": right},
            device_id_type=MESH,
        )

    arrival(agat.at[before, 0], 1).wait_recv()
    send(agat.at[before, 0], agat.at[before, 0], 5, right)
    arrival(agat.at[after, 1], 4).wait_recv()
    send(agat.at[after, 1], agat.at[after, 1], 6, left)

    lax.fori_loop(half, chunks // GROUP, second_loop, 0)

    arrival(agat.at[before, 1], 2).wait_recv()
    arrival(agat.at[after, 0], 3).wait_recv()
    for o in (1, 2, 3):
        arrival(bgat.at[lax.rem(col + X - o, X)], 6 + o).wait_recv()
    arrival(agat.at[far, 0], 5).wait_recv()
    arrival(agat.at[far, 1], 6).wait_recv()

    gains = []
    for r in range(2):
        steps = [split(agat[i, r]) for i in range(X)]
        lead = [None, steps[0]]
        offset = [jnp.zeros((block, D), F32), bgat[0, r]]
        for i in range(1, X):
            lead.append(split(dot3(steps[i], lead[i])))
            offset.append(dot3(split(offset[i]), steps[i], mm_t) + bgat[i, r])
        gains.append((lead, offset))

    @pl.when(row == 0)
    def _():
        srow[...] = jnp.zeros_like(srow)

    @pl.when(row > 0)
    def _():
        arrival(srow, 10).wait_recv()

    state = [split(srow[r]) for r in range(2)]
    for r in range(2):
        lead, offset = gains[r]
        snext[r] = dot3(state[r], lead[X], mm_t) + offset[X]
    down = remote(snext, srow, 10, below)

    @pl.when(row < rows - 1)
    def _():
        down.start()

    for r in range(2):
        lead, offset = gains[r]
        sout[0, r] = srow[r]
        for i in range(1, X):
            sout[i, r] = dot3(state[r], lead[i], mm_t) + offset[i]
    for o, target in ((1, right), (2, across), (3, left)):
        send(sout.at[lax.rem(col + o, X)], sin.at[:, here, :], 10 + o, target)
    sin[:, here, :] = sout[col]
    for o in (1, 2, 3):
        there = pl.ds(pl.multiple_of(lax.rem(col + X - o, X) * block, block), block)
        arrival(sin.at[:, there, :], 10 + o).wait_recv()

    gain = gain_ref[...]

    states = [split(sin[r]) for r in range(2)]

    def last_loop(c, _):
        span = pl.ds(pl.multiple_of(c * C, C), C)
        raws = [
            ob[r, span, :] + dot3((qah[r, span, :], qal[r, span, :]), states[r], mm_t)
            for r in range(2)
        ]
        for r in range(2):
            qf = qk[0, r, span, :].astype(F32)
            raw = raws[r] * lax.rsqrt(jnp.sum(qf * qf, axis=1, keepdims=True) + 1e-06)
            mean = jnp.sum(raw * raw, axis=1, keepdims=True) * (1.0 / D)
            g = gate_ref[r, span, :].astype(F32)
            silu = g / (1.0 + jnp.exp(-g))
            out_ref[r, span, :] = (raw * lax.rsqrt(mean + 1e-06) * gain * silu).astype(BF16)
        return 0

    lax.fori_loop(0, chunks, last_loop, 0)

    for copy in sends:
        copy.wait_send()

    @pl.when(row < rows - 1)
    def _():
        down.wait_send()


def body(query_key, values, out_gate, log_gate, strength, norm_gain):
    requests, length, _ = values.shape
    chunks = length // C
    vmem = pl.BlockSpec(memory_space=pltpu.VMEM)
    wide = (requests, chunks, C, 2 * D)
    block = D // X

    def call(*args):
        return pl.pallas_call(
            lambda *refs: kernel(chunks, *refs),
            out_shape=jax.ShapeDtypeStruct(values.shape, BF16),
            in_specs=[pl.BlockSpec(memory_space=pl.ANY)] + [vmem] * 5,
            out_specs=vmem,
            scratch_shapes=[
                pltpu.VMEM((2,) + query_key.shape, BF16),
                pltpu.VMEM((requests, chunks, C), F32),
                pltpu.VMEM((requests, chunks, C, C), F32),
                pltpu.VMEM(wide, BF16),
                pltpu.VMEM(wide, BF16),
                pltpu.VMEM((requests, chunks, D, D), BF16),
                pltpu.VMEM((requests, chunks, D, D), BF16),
                pltpu.VMEM((requests, chunks, D, D), F32),
                pltpu.VMEM((requests, chunks + 1, D, 2 * D), BF16),
                pltpu.VMEM((requests, chunks + 1, D, 2 * D), BF16),
                pltpu.VMEM((requests, length, D), BF16),
                pltpu.VMEM((requests, length, D), BF16),
                pltpu.VMEM((requests, length, D), F32),
                pltpu.VMEM((X, requests, D, D), F32),
                pltpu.VMEM((requests, D, D), F32),
                pltpu.VMEM((X, requests, block, D), F32),
                pltpu.VMEM((requests, block, D), F32),
                pltpu.VMEM((requests, block, D), F32),
                pltpu.VMEM((X, requests, block, D), F32),
                pltpu.VMEM((requests, D, D), F32),
                pltpu.SemaphoreType.DMA,
                pltpu.SemaphoreType.DMA((14,)),
                pltpu.SemaphoreType.DMA((14,)),
            ],
            compiler_params=pltpu.CompilerParams(collective_id=0, has_side_effects=True),
        )(*args)

    return call(
        query_key,
        values,
        out_gate,
        log_gate.reshape(requests, chunks, C),
        strength.reshape(requests, chunks, C),
        norm_gain.reshape(1, D),
    )


def solution(mesh):
    return jax.shard_map(
        body,
        mesh=mesh,
        in_specs=(
            P(None, "seq", "head"),
            P(None, "seq", "head"),
            P(None, "seq", "head"),
            P(None, "head", "seq"),
            P(None, "head", "seq"),
            P(),
        ),
        out_specs=P(None, "seq", "head"),
        check_vma=False,
    )
```

```python
import jax
import jax.numpy as jnp
from jax import lax
from jax.experimental import pallas as pl
from jax.experimental.pallas import tpu as pltpu
from jax.sharding import PartitionSpec as P

MESH = pl.DeviceIdType.MESH
C = 128
D = 128
X = 4
GROUP = 4
GROUPS = 2
F32 = jnp.float32
BF16 = jnp.bfloat16


def split(a):
    hi = a.astype(BF16)
    return hi, (a - hi.astype(F32)).astype(BF16)


def mm(a, b):
    return lax.dot_general(a, b, (((1,), (0,)), ((), ())), preferred_element_type=F32)


def mm_t(a, b):
    return lax.dot_general(a, b, (((1,), (1,)), ((), ())), preferred_element_type=F32)


def dot3(a, b, mul=mm):
    (ah, al), (bh, bl) = a, b
    n = ah.shape[0]
    both = mul(jnp.concatenate([ah, al], axis=0), bh)
    return both[:n] + (both[n:] + mul(ah, bl))


def dot2(a, b):
    ah, al = a
    n = ah.shape[0]
    both = mm(jnp.concatenate([ah, al], axis=0), b)
    return both[:n] + both[n:]


def iota(shape, dim):
    return lax.broadcasted_iota(jnp.int32, shape, dim)


def inverse(lows):
    lanes8 = iota((8, C), 1)
    rows8 = iota((8, C), 0)
    group8 = lanes8 // 8
    count = range(len(lows))
    packs = []
    for m in count:
        parts = [jnp.where(group8 == n, lows[m][8 * n : 8 * n + 8], 0.0) for n in range(C // 8)]
        while len(parts) > 1:
            parts = [parts[i] + parts[i + 1] for i in range(0, len(parts), 2)]
        packs.append(parts[0])
    small = [jnp.where(lanes8 - 8 * group8 == rows8, 1.0, 0.0).astype(F32)] * len(lows)
    for j in range(7):
        spot = 8 * group8 + j
        heads = [jnp.take_along_axis(packs[m], spot, axis=1, mode="promise_in_bounds") for m in count]
        small = [small[m] - heads[m] * small[m][j : j + 1] for m in count]
    rows = [[jnp.where(group8 == n, small[m], 0.0) for n in range(C // 8)] for m in count]
    b = 8
    while b < C:
        g = b // 8
        pairs = C // (2 * b)
        lane_b = iota((b, C), 1)
        zero = jnp.zeros((b, C), F32)
        offs, odds, fulls = [], [], []
        for m in count:
            off, odd = [], []
            for p in range(pairs):
                r0 = (2 * p + 1) * b
                inside = (lane_b >= 2 * p * b) & (lane_b < r0)
                off.append(jnp.where(inside, lows[m][r0 : r0 + b], 0.0))
                odd += rows[m][(2 * p + 1) * g : (2 * p + 2) * g]
            offs.append(split(jnp.concatenate(off, axis=0)))
            odds.append(jnp.concatenate(odd, axis=0))
            fulls.append(split(jnp.concatenate(rows[m], axis=0)))
        ys = [dot3(offs[m], fulls[m]) for m in count]
        spreads = []
        for m in count:
            spread = []
            for p in range(pairs):
                spread += [zero, ys[m][p * b : (p + 1) * b]]
            spreads.append(split(jnp.concatenate(spread, axis=0)))
        news = [odds[m] - dot3(split(odds[m]), spreads[m]) for m in count]
        for m in count:
            for p in range(pairs):
                for i in range(g):
                    at = (p * g + i) * 8
                    rows[m][(2 * p + 1) * g + i] = news[m][at : at + 8]
        b *= 2
    return [jnp.concatenate(rows[m], axis=0) for m in count]


def semaphores():
    names = [("swap", i) for i in range(2 * GROUPS)]
    for r in range(2):
        names += [(kind, r) for kind in ("right", "left", "far_right", "far_left")]
        names += [(kind, o, r) for kind in ("block", "state") for o in (1, 2, 3)]
        names += [("offset", s, d, r) for s in range(X) for d in range(s + 1, X)]
        names += [("gain", s, d, r) for s in range(1, X) for d in range(s + 1, X)]
    return {name: i for i, name in enumerate(names)}


SEM = semaphores()


def kernel(
    chunks,
    qk_hbm,
    values_hbm,
    gate_hbm,
    log_ref,
    write_ref,
    gain_ref,
    out_hbm,
    qk,
    values_ref,
    gate_ref,
    out_ref,
    cum,
    decay,
    wh,
    wl,
    step_h,
    step_l,
    add,
    xh,
    xl,
    qah,
    qal,
    ob,
    agat,
    bown,
    bgat,
    lead_h,
    lead_l,
    offs,
    comp,
    inv_h,
    inv_l,
    tails,
    ya,
    yb,
    srow,
    sout,
    sin,
    local_sem,
    send_sem,
    recv_sem,
):
    seq = lax.axis_index("seq")
    head = lax.axis_index("head")
    col = lax.rem(seq, X)
    row = seq // X
    base = row * X
    after = lax.rem(col + 1, X)
    far = lax.rem(col + 2, X)
    before = lax.rem(col + X - 1, X)
    right, across, left = base + after, base + far, base + before
    parity = lax.rem(head, 2)
    partner = head + 1 - 2 * parity

    barrier = pltpu.get_barrier_semaphore()
    pl.semaphore_signal(barrier, inc=1, device_id={"head": partner}, device_id_type=MESH)
    for other in (right, left, across):
        pl.semaphore_signal(barrier, inc=1, device_id={"seq": other}, device_id_type=MESH)
    for o in range(1, X):
        other = lax.rem(row + o, X) * X + col
        pl.semaphore_signal(barrier, inc=1, device_id={"seq": other}, device_id_type=MESH)
    own = pltpu.make_async_copy(qk_hbm, qk.at[parity], local_sem.at[0])
    own.start()
    take_values = pltpu.make_async_copy(values_hbm, values_ref, local_sem.at[1])
    take_values.start()
    take_gate = pltpu.make_async_copy(gate_hbm, gate_ref, local_sem.at[2])
    take_gate.start()

    tri = jnp.where(iota((C, C), 0) <= iota((C, C), 1), 1.0, 0.0).astype(F32)
    for r in range(2):
        cum[r] = lax.dot_general(
            log_ref[r],
            tri,
            (((1,), (0,)), ((), ())),
            precision=lax.Precision.HIGHEST,
            preferred_element_type=F32,
        )

    def remote(src, dst, name, target, axis="seq"):
        return pltpu.make_async_remote_copy(
            src_ref=src,
            dst_ref=dst,
            send_sem=send_sem.at[SEM[name]],
            recv_sem=recv_sem.at[SEM[name]],
            device_id={axis: target},
            device_id_type=MESH,
        )

    sends = []

    def send(*args):
        copy = remote(*args)
        copy.start()
        sends.append(copy)

    def arrive(ref, name):
        remote(ref, ref, name, right).wait_recv()

    pl.semaphore_wait(barrier, 7)
    swaps = []
    for i in range(2 * GROUPS):
        part = pl.ds(i % GROUPS * GROUP * C, GROUP * C)
        src, dst = qk_hbm.at[i // GROUPS, part, :], qk.at[parity, i // GROUPS, part, :]
        swaps.append(remote(src, dst, ("swap", i), partner, "head"))
        swaps[i].start()

    eye = iota((C, C), 0) == iota((C, C), 1)
    causal = iota((C, C), 0) >= iota((C, C), 1)
    strict = iota((C, C), 0) > iota((C, C), 1)
    ident = jnp.where(eye, 1.0, 0.0).astype(F32)
    for r in range(2):
        xh[r, 0] = jnp.concatenate([ident, jnp.zeros((C, D), F32)], axis=1).astype(BF16)
        xl[r, 0] = jnp.zeros((C, 2 * D), BF16)

    own.wait()
    take_values.wait()
    swaps[0].wait_recv()

    def first(batch, full):
        count = range(len(batch))
        ks, lows, cum_rows, rn_rows, tails_col, lasts = [], [], [], [], [], []
        for r, c in batch:
            k = qk[1, r, pl.ds(pl.multiple_of(c * C, C), C), :]
            ks.append(k)
        grams = [mm_t(k, k) for k in ks]
        for m in count:
            r, c = batch[m]
            cum_row = cum[r, pl.ds(c, 1), :]
            w_row = write_ref[r, pl.ds(c, 1), :]
            gram = grams[m]
            squares = jnp.sum(jnp.where(eye, gram, 0.0), axis=0, keepdims=True)
            rn_row = lax.rsqrt(squares + 1e-06)
            last = cum_row[:, C - 1 : C]
            tail_row = jnp.exp(last - cum_row) * w_row * rn_row
            packed = jnp.concatenate([cum_row, rn_row, tail_row, jnp.zeros((5, C), F32)], axis=0)
            cols = packed.T
            spread = jnp.exp(jnp.where(causal, cols[:, 0:1] - cum_row, -1e30)) * (w_row * rn_row)
            decay[r, c] = spread
            lows.append(jnp.where(strict, spread * gram * cols[:, 1:2], 0.0))
            cum_rows.append(cum_row)
            rn_rows.append(rn_row)
            tails_col.append(cols[:, 2:3])
            if not full:
                tails[c : c + 1, :] = tail_row
            lasts.append(last)
        invs = inverse(lows)
        scaleds = [split(invs[m] * (jnp.exp(cum_rows[m]) * rn_rows[m])) for m in count]
        invs = [split(invs[m]) for m in count]
        mixes = [dot2(scaleds[m], ks[m]) for m in count]
        if full:
            for m in count:
                r, c = batch[m]
                v = values_ref[r, pl.ds(pl.multiple_of(c * C, C), C), :]
                mixes[m] = jnp.concatenate([mixes[m], dot2(invs[m], v)], axis=1)
        for m in count:
            r, c = batch[m]
            width = mixes[m].shape[1]
            wh[r, c, :, 0:width], wl[r, c, :, 0:width] = split(mixes[m])
            uh, ul = split(mixes[m] * tails_col[m])
            kt = ks[m].T
            ab = mm(kt, uh) + mm(kt, ul)
            step_h[r, c], step_l[r, c] = split(ident * jnp.exp(lasts[m]) - ab[:, :D])
            if full:
                add[r, c] = ab[:, D:]
            else:
                inv_h[c], inv_l[c] = invs[m]

    def late(cs):
        vs = [values_ref[1, pl.ds(c * C, C), :] for c in cs]
        mixes = [dot2((inv_h[c], inv_l[c]), v) for c, v in zip(cs, vs)]
        for c, mix in zip(cs, mixes):
            col_tail = jnp.broadcast_to(tails[c : c + 1, :], (8, C)).T[:, 0:1]
            wh[1, c, :, D:], wl[1, c, :, D:] = split(mix)
            uh, ul = split(mix * col_tail)
            kt = qk[1, 1, pl.ds(c * C, C), :].T
            add[1, c] = mm(kt, uh) + mm(kt, ul)

    def scan(r, c, lo, hi):
        nxt = dot3((step_h[r, c], step_l[r, c]), (xh[r, c, :, lo:hi], xl[r, c, :, lo:hi]))
        if hi - lo == 2 * D:
            nxt = nxt + jnp.concatenate([jnp.zeros((D, D), F32), add[r, c]], axis=1)
        elif lo == D:
            nxt = nxt + add[r, c]
        xh[r, c + 1, :, lo:hi], xl[r, c + 1, :, lo:hi] = split(nxt)

    def group(g):
        return [(g // GROUPS, g % GROUPS * GROUP + j) for j in range(GROUP)]

    def stage(g):
        for r, c in group(g - 1):
            scan(r, c, 0, D if r else 2 * D)
        first(group(g), g < GROUPS)

    block = D // X
    here = pl.ds(pl.multiple_of(col * block, block), block)

    def section(r, lo):
        hi = lo + D
        return xh[r, chunks, :, lo:hi].astype(F32) + xl[r, chunks, :, lo:hi].astype(F32)

    def send_gain(r):
        agat[col, r] = section(r, 0)
        mine = agat.at[col, r]
        send(mine, mine, ("right", r), right)
        send(mine, mine, ("left", r), left)

    def send_offset(r):
        bown[r] = section(r, D).T
        for o, target in ((1, right), (2, across), (3, left)):
            there = pl.ds(pl.multiple_of(lax.rem(col + o, X) * block, block), block)
            send(bown.at[r, there, :], bgat.at[col, r], ("block", o, r), target)
        bgat[col, r] = bown[r, here, :]

    half = D // 2

    def forward(r):
        arrive(agat.at[before, r], ("right", r))
        part = agat.at[before, r, pl.ds(0, half), :]
        send(part, part, ("far_right", r), right)
        arrive(agat.at[after, r], ("left", r))
        part = agat.at[after, r, pl.ds(half, half), :]
        send(part, part, ("far_left", r), left)

    def compose(r):
        arrive(agat.at[far, r, pl.ds(0, half), :], ("far_right", r))
        arrive(agat.at[far, r, pl.ds(half, half), :], ("far_left", r))
        steps = [split(agat[i, r]) for i in range(X)]
        lead = steps[0]
        lead_h[r, 0], lead_l[r, 0] = lead
        for i in range(1, X):
            whole = dot3(steps[i], lead)
            if i < X - 1:
                lead = split(whole)
                lead_h[r, i], lead_l[r, i] = lead
            else:
                comp[r] = whole
        push(gains, r)
        for o in (1, 2, 3):
            arrive(bgat.at[lax.rem(col + X - o, X), r], ("block", o, r))
        offset = bgat[0, r]
        offs[r, 0] = offset
        for i in range(1, X):
            offset = dot3(split(offset), steps[i], mm_t) + bgat[i, r]
            offs[r, i] = offset
        push(offsets, r)

    def gains(r, s):
        if s == 0:
            return []
        return [
            remote(comp.at[r], ya.at[s - 1, r], ("gain", s, d, r), d * X + col)
            for d in range(s + 1, X)
        ]

    def offsets(r, s):
        return [
            remote(offs.at[r, X - 1], yb.at[s, r], ("offset", s, d, r), d * X + col)
            for d in range(s + 1, X)
        ]

    def push(copies, r):
        for s in range(X - 1):

            @pl.when(row == s)
            def _(s=s):
                for copy in copies(r, s):
                    copy.start()

    def settle(r):
        for d in range(X):

            @pl.when(row == d)
            def _(d=d):
                state = jnp.zeros((block, D), F32)
                for s in range(d):
                    if s == 0:
                        arrive(yb.at[0, r], ("offset", 0, d, r))
                        state = yb[0, r]
                    else:
                        arrive(ya.at[s - 1, r], ("gain", s, d, r))
                        matrix = split(ya[s - 1, r])
                        arrive(yb.at[s, r], ("offset", s, d, r))
                        state = dot3(split(state), matrix, mm_t) + yb[s, r]
                srow[r] = state

        state = split(srow[r])
        sout[0, r] = srow[r]
        for i in range(1, X):
            lead = (lead_h[r, i - 1], lead_l[r, i - 1])
            sout[i, r] = dot3(state, lead, mm_t) + offs[r, i - 1]
        for o, target in ((1, right), (2, across), (3, left)):
            dst = sin.at[r, here, :]
            send(sout.at[lax.rem(col + o, X), r], dst, ("state", o, r), target)
        sin[r, here, :] = sout[col, r]

    first(group(0), True)
    for i in range(1, 2 * GROUPS):
        swaps[i].wait_recv()
    for g in range(1, GROUPS + 1):
        stage(g)
    send_gain(0)
    send_offset(0)
    for g in range(GROUPS + 1, 2 * GROUPS):
        stage(g)
    forward(0)
    for r, c in group(2 * GROUPS - 1):
        scan(r, c, 0, D)
    send_gain(1)
    late(range(GROUP))
    for g in range(1, GROUPS):
        for j in range(GROUP):
            scan(1, (g - 1) * GROUP + j, D, 2 * D)
        late(range(g * GROUP, (g + 1) * GROUP))
    for j in range(GROUP):
        scan(1, chunks - GROUP + j, D, 2 * D)
    send_offset(1)
    forward(1)

    def second(batch):
        count = range(len(batch))
        spans = [pl.ds(pl.multiple_of(c * C, C), C) for _, c in batch]
        qs = [qk[0, batch[m][0], spans[m], :] for m in count]
        prods = [mm_t(qs[m], qk[1, batch[m][0], spans[m], :]) for m in count]
        grows, boths, leads = [], [], []
        for r, c in batch:
            packed = jnp.broadcast_to(jnp.exp(cum[r, pl.ds(c, 1), :]), (8, C))
            grows.append(packed.T[:, 0:1])
        mixings = [split(decay[batch[m]] * prods[m]) for m in count]
        boths = [dot3(mixings[m], (wh[batch[m]], wl[batch[m]])) for m in count]
        leads = [split(grows[m] * qs[m].astype(F32) - boths[m][:, :D]) for m in count]
        for m in count:
            r, c = batch[m]
            res = dot3(leads[m], (xh[r, c], xl[r, c]))
            ah, al = split(res[:, :D])
            qah[r, spans[m], :] = ah
            qal[r, spans[m], :] = al
            ob[r, spans[m], :] = boths[m][:, D:] + res[:, D:]

    compose(0)
    second(group(0))
    compose(1)
    second(group(1))
    settle(0)
    second(group(2))
    second(group(3))
    settle(1)

    gain = gain_ref[...]
    take_gate.wait()
    puts = []
    for r in range(2):
        for o in (1, 2, 3):
            there = pl.ds(pl.multiple_of(lax.rem(col + X - o, X) * block, block), block)
            arrive(sin.at[r, there, :], ("state", o, r))
        state = split(sin[r])

        def last_loop(i, _):
            spans = [pl.ds(pl.multiple_of((2 * i + j) * C, C), C) for j in range(2)]
            raws = [
                ob[r, span, :] + dot3((qah[r, span, :], qal[r, span, :]), state, mm_t)
                for span in spans
            ]
            for j in range(2):
                span = spans[j]
                qf = qk[0, r, span, :].astype(F32)
                raw = raws[j] * lax.rsqrt(jnp.sum(qf * qf, axis=1, keepdims=True) + 1e-06)
                mean = jnp.sum(raw * raw, axis=1, keepdims=True) * (1.0 / D)
                g = gate_ref[r, span, :].astype(F32)
                silu = g / (1.0 + jnp.exp(-g))
                out_ref[r, span, :] = (raw * lax.rsqrt(mean + 1e-06) * gain * silu).astype(BF16)
            return 0

        lax.fori_loop(0, chunks // 2, last_loop, 0)
        put = pltpu.make_async_copy(out_ref.at[r], out_hbm.at[r], local_sem.at[3 + r])
        put.start()
        puts.append(put)

    for copy in swaps:
        copy.wait_send()
    for copy in sends:
        copy.wait_send()
    for s in range(X - 1):

        @pl.when(row == s)
        def _(s=s):
            for r in range(2):
                for copy in gains(r, s) + offsets(r, s):
                    copy.wait_send()

    for put in puts:
        put.wait()


def body(query_key, values, out_gate, log_gate, strength, norm_gain):
    requests, length, _ = values.shape
    chunks = length // C
    vmem = pl.BlockSpec(memory_space=pltpu.VMEM)
    wide = (requests, chunks, C, 2 * D)
    block = D // X

    def call(*args):
        return pl.pallas_call(
            lambda *refs: kernel(chunks, *refs),
            out_shape=jax.ShapeDtypeStruct(values.shape, BF16),
            in_specs=[pl.BlockSpec(memory_space=pl.ANY)] * 3 + [vmem] * 3,
            out_specs=pl.BlockSpec(memory_space=pl.ANY),
            scratch_shapes=[
                pltpu.VMEM((2,) + query_key.shape, BF16),
                pltpu.VMEM(values.shape, BF16),
                pltpu.VMEM(values.shape, BF16),
                pltpu.VMEM(values.shape, BF16),
                pltpu.VMEM((requests, chunks, C), F32),
                pltpu.VMEM((requests, chunks, C, C), F32),
                pltpu.VMEM(wide, BF16),
                pltpu.VMEM(wide, BF16),
                pltpu.VMEM((requests, chunks, D, D), BF16),
                pltpu.VMEM((requests, chunks, D, D), BF16),
                pltpu.VMEM((requests, chunks, D, D), F32),
                pltpu.VMEM((requests, chunks + 1, D, 2 * D), BF16),
                pltpu.VMEM((requests, chunks + 1, D, 2 * D), BF16),
                pltpu.VMEM((requests, length, D), BF16),
                pltpu.VMEM((requests, length, D), BF16),
                pltpu.VMEM((requests, length, D), F32),
                pltpu.VMEM((X, requests, D, D), F32),
                pltpu.VMEM((requests, D, D), F32),
                pltpu.VMEM((X, requests, block, D), F32),
                pltpu.VMEM((requests, X - 1, D, D), BF16),
                pltpu.VMEM((requests, X - 1, D, D), BF16),
                pltpu.VMEM((requests, X, block, D), F32),
                pltpu.VMEM((requests, D, D), F32),
                pltpu.VMEM((chunks, C, C), BF16),
                pltpu.VMEM((chunks, C, C), BF16),
                pltpu.VMEM((chunks, C), F32),
                pltpu.VMEM((X - 2, requests, D, D), F32),
                pltpu.VMEM((X - 1, requests, block, D), F32),
                pltpu.VMEM((requests, block, D), F32),
                pltpu.VMEM((X, requests, block, D), F32),
                pltpu.VMEM((requests, D, D), F32),
                pltpu.SemaphoreType.DMA((5,)),
                pltpu.SemaphoreType.DMA((len(SEM),)),
                pltpu.SemaphoreType.DMA((len(SEM),)),
            ],
            compiler_params=pltpu.CompilerParams(collective_id=0, has_side_effects=True),
        )(*args)

    return call(
        query_key,
        values,
        out_gate,
        log_gate.reshape(requests, chunks, C),
        strength.reshape(requests, chunks, C),
        norm_gain.reshape(1, D),
    )


def solution(mesh):
    return jax.shard_map(
        body,
        mesh=mesh,
        in_specs=(
            P(None, "seq", "head"),
            P(None, "seq", "head"),
            P(None, "seq", "head"),
            P(None, "head", "seq"),
            P(None, "head", "seq"),
            P(),
        ),
        out_specs=P(None, "seq", "head"),
        check_vma=False,
    )
```

```python
import jax
import jax.numpy as jnp
from jax import lax
from jax.experimental import pallas as pl
from jax.experimental.pallas import tpu as pltpu
from jax.sharding import PartitionSpec as P

MESH = pl.DeviceIdType.MESH
C = 128
D = 128
X = 4
GROUP = 4
GROUPS = 2
SMALL = 16
F32 = jnp.float32
BF16 = jnp.bfloat16


def split(a):
    hi = a.astype(BF16)
    return hi, (a - hi.astype(F32)).astype(BF16)


def mm(a, b):
    return lax.dot_general(a, b, (((1,), (0,)), ((), ())), preferred_element_type=F32)


def mm_t(a, b):
    return lax.dot_general(a, b, (((1,), (1,)), ((), ())), preferred_element_type=F32)


def dot3(a, b, mul=mm):
    (ah, al), (bh, bl) = a, b
    n = ah.shape[0]
    both = mul(jnp.concatenate([ah, al], axis=0), bh)
    return both[:n] + (both[n:] + mul(ah, bl))


def dot2(a, b):
    ah, al = a
    n = ah.shape[0]
    both = mm(jnp.concatenate([ah, al], axis=0), b)
    return both[:n] + both[n:]


def iota(shape, dim):
    return lax.broadcasted_iota(jnp.int32, shape, dim)


def inverse(lows):
    lanes = iota((8, C), 1)
    octet = iota((8, C), 0)
    patch = lanes // SMALL
    inside = lanes - SMALL * patch
    count = range(len(lows))
    levels = SMALL // 8
    blocks = C // SMALL
    packs = []
    for m in count:
        pack = []
        for q in range(levels):
            total = None
            for n in range(blocks):
                at = SMALL * n + 8 * q
                part = jnp.where(patch == n, lows[m][at : at + 8], 0.0)
                total = part if total is None else total + part
            pack.append(total)
        packs.append(pack)
    unit = [jnp.where(inside == octet + 8 * q, 1.0, 0.0).astype(F32) for q in range(levels)]
    small = [list(unit) for _ in count]
    for j in range(SMALL - 1):
        spot = SMALL * patch + j
        for m in count:
            pivot = small[m][j // 8][j % 8 : j % 8 + 1]
            for q in range((j + 1) // 8, levels):
                head = jnp.take_along_axis(packs[m][q], spot, axis=1, mode="promise_in_bounds")
                small[m][q] = small[m][q] - head * pivot
    rows = [
        [jnp.where(patch == n, small[m][q], 0.0) for n in range(blocks) for q in range(levels)]
        for m in count
    ]
    b = SMALL
    while b < C:
        g = b // 8
        pairs = C // (2 * b)
        lane_b = iota((b, C), 1)
        zero = jnp.zeros((b, C), F32)
        offs, odds, fulls = [], [], []
        for m in count:
            off, odd = [], []
            for p in range(pairs):
                r0 = (2 * p + 1) * b
                inside = (lane_b >= 2 * p * b) & (lane_b < r0)
                off.append(jnp.where(inside, lows[m][r0 : r0 + b], 0.0))
                odd += rows[m][(2 * p + 1) * g : (2 * p + 2) * g]
            offs.append(split(jnp.concatenate(off, axis=0)))
            odds.append(jnp.concatenate(odd, axis=0))
            fulls.append(split(jnp.concatenate(rows[m], axis=0)))
        ys = [dot3(offs[m], fulls[m]) for m in count]
        spreads = []
        for m in count:
            spread = []
            for p in range(pairs):
                spread += [zero, ys[m][p * b : (p + 1) * b]]
            spreads.append(split(jnp.concatenate(spread, axis=0)))
        news = [odds[m] - dot3(split(odds[m]), spreads[m]) for m in count]
        for m in count:
            for p in range(pairs):
                for i in range(g):
                    at = (p * g + i) * 8
                    rows[m][(2 * p + 1) * g + i] = news[m][at : at + 8]
        b *= 2
    return [jnp.concatenate(rows[m], axis=0) for m in count]


def semaphores():
    names = [("swap", i) for i in range(2 * GROUPS)]
    for r in range(2):
        names += [(kind, r) for kind in ("right", "right2", "left", "left2", "far_right", "far_left")]
        names += [(kind, o, r) for kind in ("block", "state") for o in (1, 2, 3)]
        names += [("offset", s, d, r) for s in range(X) for d in range(s + 1, X)]
        names += [("gain", s, d, r) for s in range(1, X) for d in range(s + 1, X)]
    return {name: i for i, name in enumerate(names)}


SEM = semaphores()


def kernel(
    chunks,
    qk_hbm,
    values_hbm,
    gate_hbm,
    log_ref,
    write_ref,
    gain_ref,
    out_hbm,
    qk,
    values_ref,
    gate_ref,
    out_ref,
    cum,
    decay,
    wh,
    wl,
    step_h,
    step_l,
    add,
    xh,
    xl,
    qah,
    qal,
    ob,
    amp,
    agat,
    bown,
    bgat,
    lead_h,
    lead_l,
    offs,
    comp,
    inv_h,
    inv_l,
    tails,
    ya,
    yb,
    srow,
    sout,
    sin,
    local_sem,
    send_sem,
    recv_sem,
):
    seq = lax.axis_index("seq")
    head = lax.axis_index("head")
    col = lax.rem(seq, X)
    row = seq // X
    base = row * X
    after = lax.rem(col + 1, X)
    far = lax.rem(col + 2, X)
    before = lax.rem(col + X - 1, X)
    right, across, left = base + after, base + far, base + before
    parity = lax.rem(head, 2)
    partner = head + 1 - 2 * parity

    barrier = pltpu.get_barrier_semaphore()
    pl.semaphore_signal(barrier, inc=1, device_id={"head": partner}, device_id_type=MESH)
    for other in (right, left, across):
        pl.semaphore_signal(barrier, inc=1, device_id={"seq": other}, device_id_type=MESH)
    for o in range(1, X):
        other = lax.rem(row + o, X) * X + col
        pl.semaphore_signal(barrier, inc=1, device_id={"seq": other}, device_id_type=MESH)
    own = pltpu.make_async_copy(qk_hbm, qk.at[parity], local_sem.at[0])
    own.start()
    take_values = pltpu.make_async_copy(values_hbm, values_ref, local_sem.at[1])
    take_values.start()
    take_gate = pltpu.make_async_copy(gate_hbm, gate_ref, local_sem.at[2])
    take_gate.start()

    tri = jnp.where(iota((C, C), 0) <= iota((C, C), 1), 1.0, 0.0).astype(F32)
    for r in range(2):
        cum[r] = lax.dot_general(
            log_ref[r],
            tri,
            (((1,), (0,)), ((), ())),
            precision=lax.Precision.HIGHEST,
            preferred_element_type=F32,
        )

    def remote(src, dst, name, target, axis="seq"):
        return pltpu.make_async_remote_copy(
            src_ref=src,
            dst_ref=dst,
            send_sem=send_sem.at[SEM[name]],
            recv_sem=recv_sem.at[SEM[name]],
            device_id={axis: target},
            device_id_type=MESH,
        )

    sends = []

    def send(*args):
        copy = remote(*args)
        copy.start()
        sends.append(copy)

    def arrive(ref, name):
        remote(ref, ref, name, right).wait_recv()

    pl.semaphore_wait(barrier, 7)
    swaps = []
    for i in range(2 * GROUPS):
        part = pl.ds(i % GROUPS * GROUP * C, GROUP * C)
        src, dst = qk_hbm.at[i // GROUPS, part, :], qk.at[parity, i // GROUPS, part, :]
        swaps.append(remote(src, dst, ("swap", i), partner, "head"))
        swaps[i].start()

    eye = iota((C, C), 0) == iota((C, C), 1)
    causal = iota((C, C), 0) >= iota((C, C), 1)
    strict = iota((C, C), 0) > iota((C, C), 1)
    ident = jnp.where(eye, 1.0, 0.0).astype(F32)
    for r in range(2):
        xh[r, 0] = jnp.concatenate([ident, jnp.zeros((C, D), F32)], axis=1).astype(BF16)
        xl[r, 0] = jnp.zeros((C, 2 * D), BF16)

    own.wait()
    take_values.wait()
    swaps[0].wait_recv()

    def first(batch, full):
        count = range(len(batch))
        ks, lows, cum_rows, rn_rows, tails_col, lasts = [], [], [], [], [], []
        for r, c in batch:
            k = qk[1, r, pl.ds(pl.multiple_of(c * C, C), C), :]
            ks.append(k)
        grams = [mm_t(k, k) for k in ks]
        for m in count:
            r, c = batch[m]
            cum_row = cum[r, pl.ds(c, 1), :]
            w_row = write_ref[r, pl.ds(c, 1), :]
            gram = grams[m]
            squares = jnp.sum(jnp.where(eye, gram, 0.0), axis=0, keepdims=True)
            rn_row = lax.rsqrt(squares + 1e-06)
            last = cum_row[:, C - 1 : C]
            tail_row = jnp.exp(last - cum_row) * w_row * rn_row
            packed = jnp.concatenate([cum_row, rn_row, tail_row, jnp.zeros((5, C), F32)], axis=0)
            cols = packed.T
            spread = jnp.exp(jnp.where(causal, cols[:, 0:1] - cum_row, -1e30)) * (w_row * rn_row)
            decay[r, c] = spread
            lows.append(jnp.where(strict, spread * gram * cols[:, 1:2], 0.0))
            cum_rows.append(cum_row)
            rn_rows.append(rn_row)
            tails_col.append(cols[:, 2:3])
            if not full:
                tails[c : c + 1, :] = tail_row
            lasts.append(last)
        invs = inverse(lows)
        scaleds = [split(invs[m] * (jnp.exp(cum_rows[m]) * rn_rows[m])) for m in count]
        invs = [split(invs[m]) for m in count]
        mixes = [dot2(scaleds[m], ks[m]) for m in count]
        if full:
            for m in count:
                r, c = batch[m]
                v = values_ref[r, pl.ds(pl.multiple_of(c * C, C), C), :]
                mixes[m] = jnp.concatenate([mixes[m], dot2(invs[m], v)], axis=1)
        for m in count:
            r, c = batch[m]
            width = mixes[m].shape[1]
            wh[r, c, :, 0:width], wl[r, c, :, 0:width] = split(mixes[m])
            uh, ul = split(mixes[m] * tails_col[m])
            kt = ks[m].T
            ab = mm(kt, uh) + mm(kt, ul)
            step_h[r, c], step_l[r, c] = split(ident * jnp.exp(lasts[m]) - ab[:, :D])
            if full:
                add[r, c] = ab[:, D:]
            else:
                inv_h[c], inv_l[c] = invs[m]

    def late(cs):
        vs = [values_ref[1, pl.ds(c * C, C), :] for c in cs]
        mixes = [dot2((inv_h[c], inv_l[c]), v) for c, v in zip(cs, vs)]
        for c, mix in zip(cs, mixes):
            col_tail = jnp.broadcast_to(tails[c : c + 1, :], (8, C)).T[:, 0:1]
            wh[1, c, :, D:], wl[1, c, :, D:] = split(mix)
            uh, ul = split(mix * col_tail)
            kt = qk[1, 1, pl.ds(c * C, C), :].T
            add[1, c] = mm(kt, uh) + mm(kt, ul)

    def scan(r, c, lo, hi):
        nxt = dot3((step_h[r, c], step_l[r, c]), (xh[r, c, :, lo:hi], xl[r, c, :, lo:hi]))
        if hi - lo == 2 * D:
            nxt = nxt + jnp.concatenate([jnp.zeros((D, D), F32), add[r, c]], axis=1)
        elif lo == D:
            nxt = nxt + add[r, c]
        xh[r, c + 1, :, lo:hi], xl[r, c + 1, :, lo:hi] = split(nxt)

    def group(g):
        return [(g // GROUPS, g % GROUPS * GROUP + j) for j in range(GROUP)]

    def stage(g):
        for r, c in group(g - 1):
            scan(r, c, 0, D if r else 2 * D)
        first(group(g), g < GROUPS)

    block = D // X
    here = pl.ds(pl.multiple_of(col * block, block), block)

    def section(r, lo):
        hi = lo + D
        return xh[r, chunks, :, lo:hi].astype(F32) + xl[r, chunks, :, lo:hi].astype(F32)

    def send_gain(r):
        agat[col, r] = section(r, 0)
        top, low = (agat.at[col, r, pl.ds(i * half, half), :] for i in range(2))
        send(top, top, ("right", r), right)
        send(low, low, ("left", r), left)
        send(low, low, ("right2", r), right)
        send(top, top, ("left2", r), left)

    def send_offset(r):
        bown[r] = section(r, D).T
        for o, target in ((1, right), (2, across), (3, left)):
            there = pl.ds(pl.multiple_of(lax.rem(col + o, X) * block, block), block)
            send(bown.at[r, there, :], bgat.at[col, r], ("block", o, r), target)
        bgat[col, r] = bown[r, here, :]

    half = D // 2

    def forward(r):
        part = agat.at[before, r, pl.ds(0, half), :]
        arrive(part, ("right", r))
        send(part, part, ("far_right", r), right)
        part = agat.at[after, r, pl.ds(half, half), :]
        arrive(part, ("left", r))
        send(part, part, ("far_left", r), left)

    def compose(r):
        arrive(agat.at[before, r, pl.ds(half, half), :], ("right2", r))
        arrive(agat.at[after, r, pl.ds(0, half), :], ("left2", r))
        arrive(agat.at[far, r, pl.ds(0, half), :], ("far_right", r))
        arrive(agat.at[far, r, pl.ds(half, half), :], ("far_left", r))
        steps = [split(agat[i, r]) for i in range(X)]
        lead = steps[0]
        lead_h[r, 0], lead_l[r, 0] = lead
        for i in range(1, X):
            whole = dot3(steps[i], lead)
            if i < X - 1:
                lead = split(whole)
                lead_h[r, i], lead_l[r, i] = lead
            else:
                comp[r] = whole
        push(gains, r)
        for o in (1, 2, 3):
            arrive(bgat.at[lax.rem(col + X - o, X), r], ("block", o, r))
        offset = bgat[0, r]
        offs[r, 0] = offset
        for i in range(1, X):
            offset = dot3(split(offset), steps[i], mm_t) + bgat[i, r]
            offs[r, i] = offset
        push(offsets, r)

    def gains(r, s):
        if s == 0:
            return []
        return [
            remote(comp.at[r], ya.at[s - 1, r], ("gain", s, d, r), d * X + col)
            for d in range(s + 1, X)
        ]

    def offsets(r, s):
        return [
            remote(offs.at[r, X - 1], yb.at[s, r], ("offset", s, d, r), d * X + col)
            for d in range(s + 1, X)
        ]

    def push(copies, r):
        for s in range(X - 1):

            @pl.when(row == s)
            def _(s=s):
                for copy in copies(r, s):
                    copy.start()

    def settle(r):
        for d in range(X):

            @pl.when(row == d)
            def _(d=d):
                state = jnp.zeros((block, D), F32)
                for s in range(d):
                    if s == 0:
                        arrive(yb.at[0, r], ("offset", 0, d, r))
                        state = yb[0, r]
                    else:
                        arrive(ya.at[s - 1, r], ("gain", s, d, r))
                        matrix = split(ya[s - 1, r])
                        arrive(yb.at[s, r], ("offset", s, d, r))
                        state = dot3(split(state), matrix, mm_t) + yb[s, r]
                srow[r] = state

        state = split(srow[r])
        sout[0, r] = srow[r]
        for i in range(1, X):
            lead = (lead_h[r, i - 1], lead_l[r, i - 1])
            sout[i, r] = dot3(state, lead, mm_t) + offs[r, i - 1]
        for o, target in ((1, right), (2, across), (3, left)):
            dst = sin.at[r, here, :]
            send(sout.at[lax.rem(col + o, X), r], dst, ("state", o, r), target)
        sin[r, here, :] = sout[col, r]

    first(group(0), True)
    for i in range(1, 2 * GROUPS):
        swaps[i].wait_recv()
    for g in range(1, GROUPS + 1):
        stage(g)
    send_gain(0)
    send_offset(0)
    for g in range(GROUPS + 1, 2 * GROUPS):
        stage(g)
    forward(0)
    for r, c in group(2 * GROUPS - 1):
        scan(r, c, 0, D)
    send_gain(1)
    late(range(GROUP))
    for g in range(1, GROUPS):
        for j in range(GROUP):
            scan(1, (g - 1) * GROUP + j, D, 2 * D)
        late(range(g * GROUP, (g + 1) * GROUP))
    for j in range(GROUP):
        scan(1, chunks - GROUP + j, D, 2 * D)
    send_offset(1)
    forward(1)

    def second(batch):
        count = range(len(batch))
        spans = [pl.ds(pl.multiple_of(c * C, C), C) for _, c in batch]
        qs = [qk[0, batch[m][0], spans[m], :] for m in count]
        prods = [mm_t(qs[m], qk[1, batch[m][0], spans[m], :]) for m in count]
        grows, boths, leads = [], [], []
        for r, c in batch:
            packed = jnp.broadcast_to(jnp.exp(cum[r, pl.ds(c, 1), :]), (8, C))
            grows.append(packed.T[:, 0:1])
        mixings = [split(decay[batch[m]] * prods[m]) for m in count]
        boths = [dot3(mixings[m], (wh[batch[m]], wl[batch[m]])) for m in count]
        leads = [split(grows[m] * qs[m].astype(F32) - boths[m][:, :D]) for m in count]
        for m in count:
            r, c = batch[m]
            res = dot3(leads[m], (xh[r, c], xl[r, c]))
            qf = qs[m].astype(F32)
            norm = lax.rsqrt(jnp.sum(qf * qf, axis=1, keepdims=True) + 1e-06)
            qah[r, spans[m], :], qal[r, spans[m], :] = split(res[:, :D] * norm)
            ob[r, spans[m], :] = (boths[m][:, D:] + res[:, D:]) * norm
            g = gate_ref[r, spans[m], :].astype(F32)
            amp[r, spans[m], :] = gain * (g / (1.0 + jnp.exp(-g)))

    compose(0)
    take_gate.wait()
    gain = gain_ref[...]
    second(group(0))
    compose(1)
    second(group(1))
    settle(0)
    second(group(2))
    second(group(3))
    settle(1)

    puts = []
    for r in range(2):
        for o in (1, 2, 3):
            there = pl.ds(pl.multiple_of(lax.rem(col + X - o, X) * block, block), block)
            arrive(sin.at[r, there, :], ("state", o, r))
        state = split(sin[r])

        for i in range(GROUPS):
            spans = [pl.ds((i * GROUP + j) * C, C) for j in range(GROUP)]
            raws = [
                ob[r, span, :] + dot3((qah[r, span, :], qal[r, span, :]), state, mm_t)
                for span in spans
            ]
            means = [jnp.sum(raw * raw, axis=1, keepdims=True) * (1.0 / D) for raw in raws]
            for raw, mean, span in zip(raws, means, spans):
                out_ref[r, span, :] = (raw * lax.rsqrt(mean + 1e-06) * amp[r, span, :]).astype(BF16)
            part = pl.ds(i * GROUP * C, GROUP * C)
            put = pltpu.make_async_copy(
                out_ref.at[r, part, :], out_hbm.at[r, part, :], local_sem.at[3 + GROUPS * r + i]
            )
            put.start()
            puts.append(put)

    for copy in swaps:
        copy.wait_send()
    for copy in sends:
        copy.wait_send()
    for s in range(X - 1):

        @pl.when(row == s)
        def _(s=s):
            for r in range(2):
                for copy in gains(r, s) + offsets(r, s):
                    copy.wait_send()

    for put in puts:
        put.wait()


def body(query_key, values, out_gate, log_gate, strength, norm_gain):
    requests, length, _ = values.shape
    chunks = length // C
    vmem = pl.BlockSpec(memory_space=pltpu.VMEM)
    wide = (requests, chunks, C, 2 * D)
    block = D // X

    def call(*args):
        return pl.pallas_call(
            lambda *refs: kernel(chunks, *refs),
            out_shape=jax.ShapeDtypeStruct(values.shape, BF16),
            in_specs=[pl.BlockSpec(memory_space=pl.ANY)] * 3 + [vmem] * 3,
            out_specs=pl.BlockSpec(memory_space=pl.ANY),
            scratch_shapes=[
                pltpu.VMEM((2,) + query_key.shape, BF16),
                pltpu.VMEM(values.shape, BF16),
                pltpu.VMEM(values.shape, BF16),
                pltpu.VMEM(values.shape, BF16),
                pltpu.VMEM((requests, chunks, C), F32),
                pltpu.VMEM((requests, chunks, C, C), F32),
                pltpu.VMEM(wide, BF16),
                pltpu.VMEM(wide, BF16),
                pltpu.VMEM((requests, chunks, D, D), BF16),
                pltpu.VMEM((requests, chunks, D, D), BF16),
                pltpu.VMEM((requests, chunks, D, D), F32),
                pltpu.VMEM((requests, chunks + 1, D, 2 * D), BF16),
                pltpu.VMEM((requests, chunks + 1, D, 2 * D), BF16),
                pltpu.VMEM((requests, length, D), BF16),
                pltpu.VMEM((requests, length, D), BF16),
                pltpu.VMEM((requests, length, D), F32),
                pltpu.VMEM((requests, length, D), F32),
                pltpu.VMEM((X, requests, D, D), F32),
                pltpu.VMEM((requests, D, D), F32),
                pltpu.VMEM((X, requests, block, D), F32),
                pltpu.VMEM((requests, X - 1, D, D), BF16),
                pltpu.VMEM((requests, X - 1, D, D), BF16),
                pltpu.VMEM((requests, X, block, D), F32),
                pltpu.VMEM((requests, D, D), F32),
                pltpu.VMEM((chunks, C, C), BF16),
                pltpu.VMEM((chunks, C, C), BF16),
                pltpu.VMEM((chunks, C), F32),
                pltpu.VMEM((X - 2, requests, D, D), F32),
                pltpu.VMEM((X - 1, requests, block, D), F32),
                pltpu.VMEM((requests, block, D), F32),
                pltpu.VMEM((X, requests, block, D), F32),
                pltpu.VMEM((requests, D, D), F32),
                pltpu.SemaphoreType.DMA((3 + 2 * GROUPS,)),
                pltpu.SemaphoreType.DMA((len(SEM),)),
                pltpu.SemaphoreType.DMA((len(SEM),)),
            ],
            compiler_params=pltpu.CompilerParams(collective_id=0, has_side_effects=True),
        )(*args)

    return call(
        query_key,
        values,
        out_gate,
        log_gate.reshape(requests, chunks, C),
        strength.reshape(requests, chunks, C),
        norm_gain.reshape(1, D),
    )


def solution(mesh):
    return jax.shard_map(
        body,
        mesh=mesh,
        in_specs=(
            P(None, "seq", "head"),
            P(None, "seq", "head"),
            P(None, "seq", "head"),
            P(None, "head", "seq"),
            P(None, "head", "seq"),
            P(),
        ),
        out_specs=P(None, "seq", "head"),
        check_vma=False,
    )
```

```python
import jax
import jax.numpy as jnp
from jax import lax
from jax.experimental import pallas as pl
from jax.experimental.pallas import tpu as pltpu
from jax.sharding import PartitionSpec as P

MESH = pl.DeviceIdType.MESH
C = 128
D = 128
X = 4
GROUP = 4
GROUPS = 2
SMALL = 16
F32 = jnp.float32
BF16 = jnp.bfloat16


def split(a):
    hi = a.astype(BF16)
    return hi, (a - hi.astype(F32)).astype(BF16)


def mm(a, b):
    return lax.dot_general(a, b, (((1,), (0,)), ((), ())), preferred_element_type=F32)


def mm_t(a, b):
    return lax.dot_general(a, b, (((1,), (1,)), ((), ())), preferred_element_type=F32)


def dot3(a, b, mul=mm):
    (ah, al), (bh, bl) = a, b
    n = ah.shape[0]
    both = mul(jnp.concatenate([ah, al], axis=0), bh)
    return both[:n] + (both[n:] + mul(ah, bl))


def dot2(a, b):
    ah, al = a
    n = ah.shape[0]
    both = mm(jnp.concatenate([ah, al], axis=0), b)
    return both[:n] + both[n:]


def iota(shape, dim):
    return lax.broadcasted_iota(jnp.int32, shape, dim)


def inverse(lows):
    lanes = iota((8, C), 1)
    octet = iota((8, C), 0)
    patch = lanes // SMALL
    inside = lanes - SMALL * patch
    count = range(len(lows))
    levels = SMALL // 8
    blocks = C // SMALL
    packs = []
    for m in count:
        pack = []
        for q in range(levels):
            total = None
            for n in range(blocks):
                at = SMALL * n + 8 * q
                part = jnp.where(patch == n, lows[m][at : at + 8], 0.0)
                total = part if total is None else total + part
            pack.append(total)
        packs.append(pack)
    unit = [jnp.where(inside == octet + 8 * q, 1.0, 0.0).astype(F32) for q in range(levels)]
    small = [list(unit) for _ in count]
    for j in range(SMALL - 1):
        spot = SMALL * patch + j
        for m in count:
            pivot = small[m][j // 8][j % 8 : j % 8 + 1]
            for q in range((j + 1) // 8, levels):
                head = jnp.take_along_axis(packs[m][q], spot, axis=1, mode="promise_in_bounds")
                small[m][q] = small[m][q] - head * pivot
    rows = [
        [jnp.where(patch == n, small[m][q], 0.0) for n in range(blocks) for q in range(levels)]
        for m in count
    ]
    b = SMALL
    while b < C:
        g = b // 8
        pairs = C // (2 * b)
        lane_b = iota((b, C), 1)
        zero = jnp.zeros((b, C), F32)
        offs, odds, fulls = [], [], []
        for m in count:
            off, odd = [], []
            for p in range(pairs):
                r0 = (2 * p + 1) * b
                inside = (lane_b >= 2 * p * b) & (lane_b < r0)
                off.append(jnp.where(inside, lows[m][r0 : r0 + b], 0.0))
                odd += rows[m][(2 * p + 1) * g : (2 * p + 2) * g]
            offs.append(split(jnp.concatenate(off, axis=0)))
            odds.append(jnp.concatenate(odd, axis=0))
            fulls.append(split(jnp.concatenate(rows[m], axis=0)))
        ys = [dot3(offs[m], fulls[m]) for m in count]
        spreads = []
        for m in count:
            spread = []
            for p in range(pairs):
                spread += [zero, ys[m][p * b : (p + 1) * b]]
            spreads.append(split(jnp.concatenate(spread, axis=0)))
        news = [odds[m] - dot3(split(odds[m]), spreads[m]) for m in count]
        for m in count:
            for p in range(pairs):
                for i in range(g):
                    at = (p * g + i) * 8
                    rows[m][(2 * p + 1) * g + i] = news[m][at : at + 8]
        b *= 2
    return [jnp.concatenate(rows[m], axis=0) for m in count]


def semaphores():
    names = [("swap", i) for i in range(2 * GROUPS)]
    for r in range(2):
        names += [(kind, r) for kind in ("right", "right2", "left", "left2", "far_right", "far_left")]
        names += [(kind, o, r) for kind in ("block", "state") for o in (1, 2, 3)]
        names += [("offset", s, d, r) for s in range(X) for d in range(s + 1, X)]
        names += [("gain", s, d, r) for s in range(1, X) for d in range(s + 1, X)]
    return {name: i for i, name in enumerate(names)}


SEM = semaphores()


def kernel(
    chunks,
    qk_hbm,
    values_hbm,
    gate_hbm,
    log_ref,
    write_ref,
    gain_ref,
    out_hbm,
    qk,
    values_ref,
    gate_ref,
    out_ref,
    cum,
    decay,
    wh,
    wl,
    step_h,
    step_l,
    add,
    xh,
    xl,
    qah,
    qal,
    ob,
    amp,
    agat,
    bown,
    bgat,
    lead_h,
    lead_l,
    offs,
    comp,
    inv_h,
    inv_l,
    tails,
    ya,
    yb,
    srow,
    sout,
    sin,
    local_sem,
    send_sem,
    recv_sem,
):
    seq = lax.axis_index("seq")
    head = lax.axis_index("head")
    col = lax.rem(seq, X)
    row = seq // X
    base = row * X
    after = lax.rem(col + 1, X)
    far = lax.rem(col + 2, X)
    before = lax.rem(col + X - 1, X)
    right, across, left = base + after, base + far, base + before
    parity = lax.rem(head, 2)
    partner = head + 1 - 2 * parity

    barrier = pltpu.get_barrier_semaphore()
    pl.semaphore_signal(barrier, inc=1, device_id={"head": partner}, device_id_type=MESH)
    for other in (right, left, across):
        pl.semaphore_signal(barrier, inc=1, device_id={"seq": other}, device_id_type=MESH)
    for o in range(1, X):
        other = lax.rem(row + o, X) * X + col
        pl.semaphore_signal(barrier, inc=1, device_id={"seq": other}, device_id_type=MESH)
    own = pltpu.make_async_copy(qk_hbm, qk.at[parity], local_sem.at[0])
    own.start()
    take_values = pltpu.make_async_copy(values_hbm, values_ref, local_sem.at[1])
    take_values.start()
    take_gate = pltpu.make_async_copy(gate_hbm, gate_ref, local_sem.at[2])
    take_gate.start()

    tri = jnp.where(iota((C, C), 0) <= iota((C, C), 1), 1.0, 0.0).astype(F32)
    for r in range(2):
        cum[r] = lax.dot_general(
            log_ref[r],
            tri,
            (((1,), (0,)), ((), ())),
            precision=lax.Precision.HIGHEST,
            preferred_element_type=F32,
        )

    def remote(src, dst, name, target, axis="seq"):
        return pltpu.make_async_remote_copy(
            src_ref=src,
            dst_ref=dst,
            send_sem=send_sem.at[SEM[name]],
            recv_sem=recv_sem.at[SEM[name]],
            device_id={axis: target},
            device_id_type=MESH,
        )

    sends = []

    def send(*args):
        copy = remote(*args)
        copy.start()
        sends.append(copy)

    def arrive(ref, name):
        remote(ref, ref, name, right).wait_recv()

    pl.semaphore_wait(barrier, 7)
    swaps = []
    for i in range(2 * GROUPS):
        part = pl.ds(i % GROUPS * GROUP * C, GROUP * C)
        src, dst = qk_hbm.at[i // GROUPS, part, :], qk.at[parity, i // GROUPS, part, :]
        swaps.append(remote(src, dst, ("swap", i), partner, "head"))
        swaps[i].start()

    eye = iota((C, C), 0) == iota((C, C), 1)
    causal = iota((C, C), 0) >= iota((C, C), 1)
    strict = iota((C, C), 0) > iota((C, C), 1)
    ident = jnp.where(eye, 1.0, 0.0).astype(F32)
    for r in range(2):
        xh[r, 0] = jnp.concatenate([ident, jnp.zeros((C, D), F32)], axis=1).astype(BF16)
        xl[r, 0] = jnp.zeros((C, 2 * D), BF16)

    own.wait()
    take_values.wait()
    swaps[0].wait_recv()

    def first(batch, full):
        count = range(len(batch))
        ks, lows, cum_rows, rn_rows, tails_col, lasts = [], [], [], [], [], []
        for r, c in batch:
            k = qk[1, r, pl.ds(pl.multiple_of(c * C, C), C), :]
            ks.append(k)
        grams = [mm_t(k, k) for k in ks]
        for m in count:
            r, c = batch[m]
            cum_row = cum[r, pl.ds(c, 1), :]
            w_row = write_ref[r, pl.ds(c, 1), :]
            gram = grams[m]
            squares = jnp.sum(jnp.where(eye, gram, 0.0), axis=0, keepdims=True)
            rn_row = lax.rsqrt(squares + 1e-06)
            last = cum_row[:, C - 1 : C]
            tail_row = jnp.exp(last - cum_row) * w_row * rn_row
            packed = jnp.concatenate([cum_row, rn_row, tail_row, jnp.zeros((5, C), F32)], axis=0)
            cols = packed.T
            spread = jnp.exp(jnp.where(causal, cols[:, 0:1] - cum_row, -1e30)) * (w_row * rn_row)
            decay[r, c] = spread
            lows.append(jnp.where(strict, spread * gram * cols[:, 1:2], 0.0))
            cum_rows.append(cum_row)
            rn_rows.append(rn_row)
            tails_col.append(cols[:, 2:3])
            if not full:
                tails[c : c + 1, :] = tail_row
            lasts.append(last)
        invs = inverse(lows)
        scaleds = [split(invs[m] * (jnp.exp(cum_rows[m]) * rn_rows[m])) for m in count]
        invs = [split(invs[m]) for m in count]
        mixes = [dot2(scaleds[m], ks[m]) for m in count]
        if full:
            for m in count:
                r, c = batch[m]
                v = values_ref[r, pl.ds(pl.multiple_of(c * C, C), C), :]
                mixes[m] = jnp.concatenate([mixes[m], dot2(invs[m], v)], axis=1)
        for m in count:
            r, c = batch[m]
            width = mixes[m].shape[1]
            wh[r, c, :, 0:width], wl[r, c, :, 0:width] = split(mixes[m])
            uh, ul = split(mixes[m] * tails_col[m])
            kt = ks[m].T
            ab = mm(kt, uh) + mm(kt, ul)
            step_h[r, c], step_l[r, c] = split(ident * jnp.exp(lasts[m]) - ab[:, :D])
            if full:
                add[r, c] = ab[:, D:]
            else:
                inv_h[c], inv_l[c] = invs[m]

    def late(cs):
        vs = [values_ref[1, pl.ds(c * C, C), :] for c in cs]
        mixes = [dot2((inv_h[c], inv_l[c]), v) for c, v in zip(cs, vs)]
        for c, mix in zip(cs, mixes):
            col_tail = jnp.broadcast_to(tails[c : c + 1, :], (8, C)).T[:, 0:1]
            wh[1, c, :, D:], wl[1, c, :, D:] = split(mix)
            uh, ul = split(mix * col_tail)
            kt = qk[1, 1, pl.ds(c * C, C), :].T
            add[1, c] = mm(kt, uh) + mm(kt, ul)

    def scan(r, c, lo, hi):
        nxt = dot3((step_h[r, c], step_l[r, c]), (xh[r, c, :, lo:hi], xl[r, c, :, lo:hi]))
        if hi - lo == 2 * D:
            nxt = nxt + jnp.concatenate([jnp.zeros((D, D), F32), add[r, c]], axis=1)
        elif lo == D:
            nxt = nxt + add[r, c]
        xh[r, c + 1, :, lo:hi], xl[r, c + 1, :, lo:hi] = split(nxt)

    def group(g):
        return [(g // GROUPS, g % GROUPS * GROUP + j) for j in range(GROUP)]

    def stage(g):
        for r, c in group(g - 1):
            scan(r, c, 0, D if r else 2 * D)
        first(group(g), g < GROUPS)

    block = D // X
    here = pl.ds(pl.multiple_of(col * block, block), block)

    def section(r, lo):
        hi = lo + D
        return xh[r, chunks, :, lo:hi].astype(F32) + xl[r, chunks, :, lo:hi].astype(F32)

    def send_gain(r):
        agat[col, r] = section(r, 0)
        top, low = (agat.at[col, r, pl.ds(i * half, half), :] for i in range(2))
        send(top, top, ("right", r), right)
        send(low, low, ("left", r), left)
        send(low, low, ("right2", r), right)
        send(top, top, ("left2", r), left)

    def send_offset(r):
        bown[r] = section(r, D).T
        for o, target in ((1, right), (2, across), (3, left)):
            there = pl.ds(pl.multiple_of(lax.rem(col + o, X) * block, block), block)
            send(bown.at[r, there, :], bgat.at[col, r], ("block", o, r), target)
        bgat[col, r] = bown[r, here, :]

    half = D // 2

    def forward(r):
        part = agat.at[before, r, pl.ds(0, half), :]
        arrive(part, ("right", r))
        send(part, part, ("far_right", r), right)
        part = agat.at[after, r, pl.ds(half, half), :]
        arrive(part, ("left", r))
        send(part, part, ("far_left", r), left)

    def compose(r):
        arrive(agat.at[before, r, pl.ds(half, half), :], ("right2", r))
        arrive(agat.at[after, r, pl.ds(0, half), :], ("left2", r))
        arrive(agat.at[far, r, pl.ds(0, half), :], ("far_right", r))
        arrive(agat.at[far, r, pl.ds(half, half), :], ("far_left", r))
        steps = [split(agat[i, r]) for i in range(X)]
        lead_h[r, 0], lead_l[r, 0] = steps[0]
        lower = split(dot3(steps[1], steps[0]))
        upper = split(dot3(steps[3], steps[2]))
        comp[r] = dot3(upper, lower)
        push(gains, r)
        lead_h[r, 1], lead_l[r, 1] = lower
        lead_h[r, 2], lead_l[r, 2] = split(dot3(steps[2], lower))
        for o in (1, 2, 3):
            arrive(bgat.at[lax.rem(col + X - o, X), r], ("block", o, r))
        offset = bgat[0, r]
        offs[r, 0] = offset
        for i in range(1, X):
            offset = dot3(split(offset), steps[i], mm_t) + bgat[i, r]
            offs[r, i] = offset
        push(offsets, r)

    def gains(r, s):
        if s == 0:
            return []
        return [
            remote(comp.at[r], ya.at[s - 1, r], ("gain", s, d, r), d * X + col)
            for d in reversed(range(s + 1, X))
        ]

    def offsets(r, s):
        return [
            remote(offs.at[r, X - 1], yb.at[s, r], ("offset", s, d, r), d * X + col)
            for d in reversed(range(s + 1, X))
        ]

    def push(copies, r):
        for s in range(X - 1):

            @pl.when(row == s)
            def _(s=s):
                for copy in copies(r, s):
                    copy.start()

    def settle(r):
        for d in range(X):

            @pl.when(row == d)
            def _(d=d):
                state = jnp.zeros((block, D), F32)
                for s in range(d):
                    if s == 0:
                        arrive(yb.at[0, r], ("offset", 0, d, r))
                        state = yb[0, r]
                    else:
                        arrive(ya.at[s - 1, r], ("gain", s, d, r))
                        matrix = split(ya[s - 1, r])
                        arrive(yb.at[s, r], ("offset", s, d, r))
                        state = dot3(split(state), matrix, mm_t) + yb[s, r]
                srow[r] = state

        state = split(srow[r])
        sout[0, r] = srow[r]
        for i in range(1, X):
            lead = (lead_h[r, i - 1], lead_l[r, i - 1])
            sout[i, r] = dot3(state, lead, mm_t) + offs[r, i - 1]
        for o, target in ((1, right), (2, across), (3, left)):
            dst = sin.at[r, here, :]
            send(sout.at[lax.rem(col + o, X), r], dst, ("state", o, r), target)
        sin[r, here, :] = sout[col, r]

    first(group(0), True)
    for i in range(1, 2 * GROUPS):
        swaps[i].wait_recv()
    for g in range(1, GROUPS + 1):
        stage(g)
    send_gain(0)
    send_offset(0)
    for g in range(GROUPS + 1, 2 * GROUPS):
        stage(g)
    forward(0)
    for r, c in group(2 * GROUPS - 1):
        scan(r, c, 0, D)
    send_gain(1)
    late(range(GROUP))
    for g in range(1, GROUPS):
        for j in range(GROUP):
            scan(1, (g - 1) * GROUP + j, D, 2 * D)
        late(range(g * GROUP, (g + 1) * GROUP))
    for j in range(GROUP):
        scan(1, chunks - GROUP + j, D, 2 * D)
    send_offset(1)
    forward(1)

    def second(batch):
        count = range(len(batch))
        spans = [pl.ds(pl.multiple_of(c * C, C), C) for _, c in batch]
        qs = [qk[0, batch[m][0], spans[m], :] for m in count]
        prods = [mm_t(qs[m], qk[1, batch[m][0], spans[m], :]) for m in count]
        grows, boths, leads = [], [], []
        for r, c in batch:
            packed = jnp.broadcast_to(jnp.exp(cum[r, pl.ds(c, 1), :]), (8, C))
            grows.append(packed.T[:, 0:1])
        mixings = [split(decay[batch[m]] * prods[m]) for m in count]
        boths = [dot3(mixings[m], (wh[batch[m]], wl[batch[m]])) for m in count]
        leads = [split(grows[m] * qs[m].astype(F32) - boths[m][:, :D]) for m in count]
        for m in count:
            r, c = batch[m]
            res = dot3(leads[m], (xh[r, c], xl[r, c]))
            qf = qs[m].astype(F32)
            norm = lax.rsqrt(jnp.sum(qf * qf, axis=1, keepdims=True) + 1e-06)
            qah[r, spans[m], :], qal[r, spans[m], :] = split(res[:, :D] * norm)
            ob[r, spans[m], :] = (boths[m][:, D:] + res[:, D:]) * norm
            g = gate_ref[r, spans[m], :].astype(F32)
            amp[r, spans[m], :] = gain * (g / (1.0 + jnp.exp(-g)))

    compose(0)
    take_gate.wait()
    gain = gain_ref[...]
    second(group(0))
    compose(1)
    second(group(1))
    second(group(2))
    settle(0)
    second(group(3))
    settle(1)

    puts = []
    for r in range(2):
        for o in (1, 2, 3):
            there = pl.ds(pl.multiple_of(lax.rem(col + X - o, X) * block, block), block)
            arrive(sin.at[r, there, :], ("state", o, r))
        state = split(sin[r])

        for i in range(GROUPS):
            spans = [pl.ds((i * GROUP + j) * C, C) for j in range(GROUP)]
            raws = [
                ob[r, span, :] + dot3((qah[r, span, :], qal[r, span, :]), state, mm_t)
                for span in spans
            ]
            means = [jnp.sum(raw * raw, axis=1, keepdims=True) * (1.0 / D) for raw in raws]
            for raw, mean, span in zip(raws, means, spans):
                out_ref[r, span, :] = (raw * lax.rsqrt(mean + 1e-06) * amp[r, span, :]).astype(BF16)
            part = pl.ds(i * GROUP * C, GROUP * C)
            put = pltpu.make_async_copy(
                out_ref.at[r, part, :], out_hbm.at[r, part, :], local_sem.at[3 + GROUPS * r + i]
            )
            put.start()
            puts.append(put)

    for copy in swaps:
        copy.wait_send()
    for copy in sends:
        copy.wait_send()
    for s in range(X - 1):

        @pl.when(row == s)
        def _(s=s):
            for r in range(2):
                for copy in gains(r, s) + offsets(r, s):
                    copy.wait_send()

    for put in puts:
        put.wait()


def body(query_key, values, out_gate, log_gate, strength, norm_gain):
    requests, length, _ = values.shape
    chunks = length // C
    vmem = pl.BlockSpec(memory_space=pltpu.VMEM)
    wide = (requests, chunks, C, 2 * D)
    block = D // X

    def call(*args):
        return pl.pallas_call(
            lambda *refs: kernel(chunks, *refs),
            out_shape=jax.ShapeDtypeStruct(values.shape, BF16),
            in_specs=[pl.BlockSpec(memory_space=pl.ANY)] * 3 + [vmem] * 3,
            out_specs=pl.BlockSpec(memory_space=pl.ANY),
            scratch_shapes=[
                pltpu.VMEM((2,) + query_key.shape, BF16),
                pltpu.VMEM(values.shape, BF16),
                pltpu.VMEM(values.shape, BF16),
                pltpu.VMEM(values.shape, BF16),
                pltpu.VMEM((requests, chunks, C), F32),
                pltpu.VMEM((requests, chunks, C, C), F32),
                pltpu.VMEM(wide, BF16),
                pltpu.VMEM(wide, BF16),
                pltpu.VMEM((requests, chunks, D, D), BF16),
                pltpu.VMEM((requests, chunks, D, D), BF16),
                pltpu.VMEM((requests, chunks, D, D), F32),
                pltpu.VMEM((requests, chunks + 1, D, 2 * D), BF16),
                pltpu.VMEM((requests, chunks + 1, D, 2 * D), BF16),
                pltpu.VMEM((requests, length, D), BF16),
                pltpu.VMEM((requests, length, D), BF16),
                pltpu.VMEM((requests, length, D), F32),
                pltpu.VMEM((requests, length, D), F32),
                pltpu.VMEM((X, requests, D, D), F32),
                pltpu.VMEM((requests, D, D), F32),
                pltpu.VMEM((X, requests, block, D), F32),
                pltpu.VMEM((requests, X - 1, D, D), BF16),
                pltpu.VMEM((requests, X - 1, D, D), BF16),
                pltpu.VMEM((requests, X, block, D), F32),
                pltpu.VMEM((requests, D, D), F32),
                pltpu.VMEM((chunks, C, C), BF16),
                pltpu.VMEM((chunks, C, C), BF16),
                pltpu.VMEM((chunks, C), F32),
                pltpu.VMEM((X - 2, requests, D, D), F32),
                pltpu.VMEM((X - 1, requests, block, D), F32),
                pltpu.VMEM((requests, block, D), F32),
                pltpu.VMEM((X, requests, block, D), F32),
                pltpu.VMEM((requests, D, D), F32),
                pltpu.SemaphoreType.DMA((3 + 2 * GROUPS,)),
                pltpu.SemaphoreType.DMA((len(SEM),)),
                pltpu.SemaphoreType.DMA((len(SEM),)),
            ],
            compiler_params=pltpu.CompilerParams(collective_id=0, has_side_effects=True),
        )(*args)

    return call(
        query_key,
        values,
        out_gate,
        log_gate.reshape(requests, chunks, C),
        strength.reshape(requests, chunks, C),
        norm_gain.reshape(1, D),
    )


def solution(mesh):
    return jax.shard_map(
        body,
        mesh=mesh,
        in_specs=(
            P(None, "seq", "head"),
            P(None, "seq", "head"),
            P(None, "seq", "head"),
            P(None, "head", "seq"),
            P(None, "head", "seq"),
            P(),
        ),
        out_specs=P(None, "seq", "head"),
        check_vma=False,
    )
```
